32 devices in a mesh: gx: 8 (over y, x, core), gy: 4 (over z).
Axes of the slice: x: 2, y: 2, z: 4, core: 2. Of those that a mesh axis runs over, the one named last changes fastest.
Arguments:
- tokens: bfloat16 [3072, 2048], P('gx', 'gy'), may hold values from -40 to 40
- gain: float32 [2048], replicated, may hold values from 0.1 to 1.9
- w_qkv: bfloat16 [2048, 3, 16, 128], P('gx', None, 'gy'), may hold values from -0.176776695 to 0.176776695
- w_out: bfloat16 [2048, 2048], P('gx', 'gy'), may hold values from -0.125 to 0.125
- lengths: int32 [6], replicated, may hold values from 1 to 2048, 3072 in all
Outputs:
- mixed: bfloat16 [3072, 2048], P('gx', 'gy')
- key_cache: bfloat16 [3072, 16, 128], P('gx', 'gy')
- value_cache: bfloat16 [3072, 16, 128], P('gx', 'gy')
The draws below stay inside these ranges and needn't reach their ends.
Inputs may be any that keep to these rules, and one draw needn't show every extreme that they name: lengths are positive and sum to 3072; the longest is exactly 2048.
All inputs are finite; a program needn't handle non-finite values.
Results may differ from the reference program's by a relative error of at most 0.012.
The reference program's roundings to bfloat16 on the way (of `normed`, `query_rot` and `attended`) count: a program that leaves them out, or rounds other values in their place, can miss the bound.
Values may be sent and summed in bfloat16 or wider, within the bound.
No kernel may reach another device: no remote copies, remote signals or barrier semaphores. Data moves between devices by JAX's collectives and lax.ppermute only.
A program may use at most 64 MiB of HBM per device.

```python
import math
import jax
import jax.numpy as jnp
import numpy as np
from jax import lax

D = 2048
H = 16
HD = 128
TOKENS = 3072
MAXLEN = 2048
NDOCS = 6


def draw_tokens(key, part):
    first, second, third = jax.random.split(key, 3)
    base = jax.random.truncated_normal(first, -4.0, 4.0, (TOKENS, D), jnp.float32)
    rows = jnp.exp(jax.random.uniform(second, (TOKENS, 1), jnp.float32) * jnp.log(10.0))
    columns = jnp.exp(jax.random.uniform(third, (1, D), jnp.float32) * jnp.log(10.0))
    return (0.1 * base * rows * columns).astype(jnp.bfloat16)


def draw_w_qkv(key, part):
    first = jax.random.fold_in(key, 0)
    fan_scale = 1.0 / math.sqrt(D)
    weights = jax.random.truncated_normal(first, -4.0, 4.0, (D, 3, H, HD), jnp.float32) * fan_scale
    return weights.astype(jnp.bfloat16)


def block_scale(own_key, shape, cuts, least, largest):
    loudness = 1.0
    for dim, blocks in cuts:
        heights = jax.random.uniform(jax.random.fold_in(jax.random.fold_in(own_key, 6), dim), (blocks,), jnp.float32, least / len(cuts), largest / len(cuts))
        loudness = loudness * jnp.repeat(jnp.exp(heights), shape[dim] // blocks).reshape((-1,) + (1,) * (len(shape) - 1 - dim))
    return loudness


def split_up(number_of, total, limit, lean):
    weights = [(1 << 20) // math.isqrt(grade ** lean) + 1 for grade in range(2, number_of + 1)]
    spare, counts = total - limit - (number_of - 1), [1] * (number_of - 1)
    while spare > 0:
        free = [i for i in range(number_of - 1) if counts[i] < limit]
        pool, budget = sum([weights[i] for i in free]), spare
        for i in free:
            addition = min(limit - counts[i], max(1, budget * weights[i] // pool), spare)
            counts[i] = counts[i] + addition
            spare = spare - addition
    return np.array([limit] + counts)


def uneven_parts(stream_key, amount, total, reach, slope):
    if amount == 2:
        one = jax.random.randint(stream_key, (), max(1, total - reach), min(reach, total - 1) + 1)
        return jnp.stack([one, total - one])
    sizes = jnp.asarray(split_up(amount, total, reach, slope), jnp.int32)
    couples = (amount - 1) // 2
    source_of, taker = sizes[1:1 + 2 * couples:2], sizes[2:2 + 2 * couples:2]
    slack = jnp.minimum(source_of - 1, reach - taker)
    moved = jax.random.randint(jax.random.fold_in(stream_key, 1), (couples,), 0, 1 << 20) % (slack + 1)
    sizes = sizes.at[1:1 + 2 * couples:2].set(source_of - moved).at[2:2 + 2 * couples:2].set(taker + moved)
    return sizes[jax.random.permutation(jax.random.fold_in(stream_key, 2), amount)]


def gaussian(stream_key, dims, spread, bound, pieces=(), held_as=jnp.bfloat16):
    level = block_scale(stream_key, dims, pieces, -0.22, 0.18) if pieces else 1.0
    entries = jax.random.normal(stream_key, dims, jnp.float32) * spread * level
    return jnp.minimum(jnp.maximum(entries, -bound), bound).astype(held_as)


def setup_inputs(seed: int = 0) -> dict:
    keys = jax.random.split(jax.random.key(seed), 6)
    tokens = draw_tokens(jax.random.fold_in(keys[5], 71), 0)
    gain = jnp.clip(1.0 + 0.18 * jax.random.normal(keys[1], (D,), jnp.float32), 0.1, 1.9)
    w_qkv = draw_w_qkv(jax.random.fold_in(keys[5], 71), 0)
    w_out = gaussian(keys[3], (D, D), D ** -0.5, 0.125, ((0, 8), (1, 4)))
    lengths = uneven_parts(keys[4], NDOCS, TOKENS, MAXLEN, 2).astype(jnp.int32)
    return {"tokens": tokens, "gain": gain, "w_qkv": w_qkv, "w_out": w_out, "lengths": lengths}


def rotate(vectors, position):
    half = HD // 2
    freq = 10000.0 ** (-(2.0 * jnp.arange(half, dtype=jnp.float32)) / HD)
    angle = position.astype(jnp.float32)[:, None, None] * freq[None, None, :]
    cosine = jnp.cos(angle)
    sine = jnp.sin(angle)
    first = vectors[..., :half]
    second = vectors[..., half:]
    return jnp.concatenate([first * cosine - second * sine, second * cosine + first * sine], axis=-1)

def reference(tokens, gain, w_qkv, w_out, lengths):
    wide = tokens.astype(jnp.float32)
    meansq = lax.optimization_barrier(jnp.mean(wide * wide, axis=-1, keepdims=True))
    normed = (wide * lax.rsqrt(meansq + 1e-06) * gain[None, :]).astype(jnp.bfloat16)
    projected = jnp.dot(normed, w_qkv.reshape(D, 3 * D), preferred_element_type=jnp.float32)
    projected = projected.reshape(TOKENS, 3, H, HD)
    index = jnp.arange(TOKENS, dtype=jnp.int32)
    doc_start = (jnp.cumsum(lengths) - lengths).astype(jnp.int32)
    begin = lax.optimization_barrier(jnp.max(jnp.where(doc_start[None, :] <= index[:, None], doc_start[None, :], 0), axis=1)).astype(jnp.int32)
    position = index - begin
    query_rot = rotate(projected[:, 0], position).astype(jnp.bfloat16)
    key_cache = rotate(projected[:, 1], position).astype(jnp.bfloat16)
    value_cache = projected[:, 2].astype(jnp.bfloat16)
    block = math.gcd(TOKENS, 1024)
    nblocks = TOKENS // block
    scale = 1.0 / math.sqrt(HD)

    def one_head(head):
        keys_h = lax.dynamic_index_in_dim(key_cache, head, 1, keepdims=False)
        vals_h = lax.dynamic_index_in_dim(value_cache, head, 1, keepdims=False)
        query_h = lax.dynamic_index_in_dim(query_rot, head, 1, keepdims=False)

        def one_block(number):
            first = (number * block).astype(jnp.int32)
            rows = lax.dynamic_slice_in_dim(query_h, first, block, 0)
            rows_begin = lax.dynamic_slice_in_dim(begin, first, block, 0)
            rows_index = first + jnp.arange(block, dtype=jnp.int32)
            score = jnp.dot(rows, keys_h.T, preferred_element_type=jnp.float32) * scale
            keep = (index[None, :] >= rows_begin[:, None]) & (index[None, :] <= rows_index[:, None])
            top = lax.optimization_barrier(jnp.max(jnp.where(keep, score, -jnp.inf), axis=1, keepdims=True))
            weight = jnp.where(keep, jnp.exp(score - top), 0.0)
            total = lax.optimization_barrier(jnp.sum(weight, axis=1, keepdims=True))
            summed = jnp.dot(weight.astype(jnp.bfloat16), vals_h, preferred_element_type=jnp.float32)
            return (summed / total).astype(jnp.bfloat16)
        return lax.map(one_block, jnp.arange(nblocks, dtype=jnp.int32)).reshape(TOKENS, HD)
    attended = lax.map(one_head, jnp.arange(H, dtype=jnp.int32))
    attended = jnp.transpose(attended, (1, 0, 2)).reshape(TOKENS, D)
    mixed = jnp.dot(attended, w_out, preferred_element_type=jnp.float32).astype(jnp.bfloat16)
    return (mixed, key_cache, value_cache)
```

```python
import functools
import math

import jax
import jax.numpy as jnp
from jax import lax
from jax.experimental import pallas as pl
from jax.experimental.pallas import tpu as pltpu
from jax.sharding import PartitionSpec as P


def tables(position, hsize):
    half = hsize // 2
    freq = 10000.0 ** (-(2.0 * jnp.arange(half, dtype=jnp.float32)) / hsize)
    angle = position.astype(jnp.float32)[:, None] * freq[None, :]
    return jnp.cos(angle), jnp.sin(angle)


def rotate(vectors, position):
    half = vectors.shape[-1] // 2
    cosine, sine = tables(position, vectors.shape[-1])
    cosine, sine = cosine[:, None, :], sine[:, None, :]
    first = vectors[..., :half]
    second = vectors[..., half:]
    return jnp.concatenate(
        [first * cosine - second * sine, second * cosine + first * sine], axis=-1
    )


def begins(lengths, glob):
    doc_start = jnp.cumsum(lengths) - lengths
    return jnp.max(jnp.where(doc_start[None, :] <= glob[:, None], doc_start[None, :], 0), axis=1)


def block_rows(count):
    size = count
    while size > 1024 and size % 2 == 0:
        size = size // 2
    return size


def general(tokens, gain, w_qkv, w_out, lengths):
    tok_dev = tokens.shape[0]
    hloc = w_qkv.shape[2]
    hsize = w_qkv.shape[3]
    whole = lax.all_gather(tokens, "gy", axis=1, tiled=True)
    wide = whole.astype(jnp.float32)
    meansq = jnp.mean(wide * wide, axis=-1, keepdims=True)
    normed = (wide * lax.rsqrt(meansq + 1e-06) * gain[None, :]).astype(jnp.bfloat16)
    piece = lax.all_gather(w_qkv, "gx", axis=0, tiled=True)
    projected = jnp.dot(
        normed, piece.reshape(piece.shape[0], -1), preferred_element_type=jnp.float32
    )
    projected = projected.reshape(tok_dev, 3, hloc, hsize)
    mine = lax.axis_index("gx")
    glob = mine * tok_dev + jnp.arange(tok_dev, dtype=jnp.int32)
    begin = begins(lengths, glob)
    position = glob - begin
    query = rotate(projected[:, 0], position).astype(jnp.bfloat16)
    keys_own = rotate(projected[:, 1], position).astype(jnp.bfloat16)
    vals_own = projected[:, 2].astype(jnp.bfloat16)
    scale = 1.0 / math.sqrt(hsize)
    initial = (
        jnp.full((hloc, tok_dev), -1e30, jnp.float32),
        jnp.zeros((hloc, tok_dev), jnp.float32),
        jnp.zeros((hloc, tok_dev, hsize), jnp.float32),
    )
    keys_piece = lax.all_gather(keys_own, "gx", axis=0, tiled=True)
    vals_piece = lax.all_gather(vals_own, "gx", axis=0, tiled=True)
    count = keys_piece.shape[0]
    size = block_rows(count)

    def one_tile(number, state):
        running, totals, accum = state
        first = (number * size).astype(jnp.int32)
        keys_blk = lax.dynamic_slice_in_dim(keys_piece, first, size, 0)
        vals_blk = lax.dynamic_slice_in_dim(vals_piece, first, size, 0)
        kidx = first + jnp.arange(size, dtype=jnp.int32)
        score = (
            jnp.einsum("qhd,khd->hqk", query, keys_blk, preferred_element_type=jnp.float32) * scale
        )
        keep = (kidx[None, :] >= begin[:, None]) & (kidx[None, :] <= glob[:, None])
        score = jnp.where(keep[None], score, -1e30)
        newmax = jnp.maximum(running, jnp.max(score, axis=-1))
        weight = jnp.where(keep[None], jnp.exp(score - newmax[..., None]), 0.0)
        factor = jnp.exp(running - newmax)
        totals = totals * factor + jnp.sum(weight, axis=-1)
        update = jnp.einsum(
            "hqk,khd->hqd",
            weight.astype(jnp.bfloat16),
            vals_blk,
            preferred_element_type=jnp.float32,
        )
        accum = accum * factor[..., None] + update
        return (newmax, totals, accum)

    running, totals, accum = lax.fori_loop(0, count // size, one_tile, initial)
    attended = (accum / totals[..., None]).astype(jnp.bfloat16)
    attended = jnp.transpose(attended, (1, 0, 2)).reshape(tok_dev, hloc * hsize)
    all_heads = lax.all_gather(attended, "gy", axis=1, tiled=True)
    mixed = jnp.dot(
        all_heads, lax.all_gather(w_out, "gx", axis=0, tiled=True),
        preferred_element_type=jnp.float32,
    ).astype(jnp.bfloat16)
    return (mixed, keys_own, vals_own)


LINE = 4
CHIPS = 4


def swap(x, mask):
    return lax.ppermute(x, "gx", [(i, i ^ mask) for i in range(2 * CHIPS)])


def up(x, least):
    return lax.ppermute(x, "gy", [(i, i + 1) for i in range(least, LINE - 1)])


def down(x, most):
    return lax.ppermute(x, "gy", [(i, i - 1) for i in range(most, 0, -1)])


def along_line(x):
    u1, d1 = up(x, 0), down(x, 3)
    u2, d2 = up(u1, 1), down(d1, 2)
    u3, d3 = up(u2, 2), down(d2, 1)
    return (u1, u2, u3), (d1, d2, d3)


def vmem():
    return pl.BlockSpec(memory_space=pltpu.VMEM)


def project_kernel(
    where_ref, own, u1, u2, u3, d1, d2, d3, gain_ref, cos_ref, sin_ref,
    wa0, wa1, wa2, wa3, wa4, wb0, wb1, wb2, wb3, wb4,
    o0, o1, o2, o3, key_ref, val_ref,
    x_ref, slot_ref,
):
    step = pl.program_id(0)
    chip, core, line = where_ref[0], where_ref[1], where_ref[2]
    wide = own.shape[1]

    @pl.when(step == 0)
    def _():
        raw = [
            own[...].astype(jnp.float32),
            jnp.where(line >= 1, u1[...], d3[...]).astype(jnp.float32),
            jnp.where(line >= 2, u2[...], d2[...]).astype(jnp.float32),
            jnp.where(line >= 3, u3[...], d1[...]).astype(jnp.float32),
        ]
        square = sum(jnp.sum(r * r, axis=1, keepdims=True) for r in raw)
        scale = lax.rsqrt(square * (1.0 / (LINE * wide)) + 1e-06)
        for d in range(LINE):
            feature = (line - d) & 3
            normed = (raw[d] * scale * gain_ref[feature]).astype(jnp.bfloat16)
            x_ref[2 * d] = normed[:, : wide // 2]
            x_ref[2 * d + 1] = normed[:, wide // 2 :]

    total = None
    for half, refs in ((core, (wa0, wa1, wa2, wa3, wa4)), (1 - core, (wb0, wb1, wb2, wb3, wb4))):
        for m in range(CHIPS):
            x = x_ref[2 * ((line - (chip ^ m)) & 3) + half]
            if m < 3:
                parts = [(x, refs[m])]
            else:
                parts = [(x[:, : wide // 4], refs[3]), (x[:, wide // 4 :], refs[4])]
            for left, right in parts:
                part = jnp.dot(left, right[...], preferred_element_type=jnp.float32)
                total = part if total is None else total + part

    hsize = cos_ref.shape[1]

    @pl.when(step < 2)
    def _():
        for h in range(CHIPS):
            u = total[:, h * hsize : (h + 1) * hsize]
            u = u * cos_ref[...] + pltpu.roll(u, hsize // 2, 1) * sin_ref[...]
            slot_ref[h] = u.astype(jnp.bfloat16)

    @pl.when(step == 2)
    def _():
        for h in range(CHIPS):
            slot_ref[h] = total[:, h * hsize : (h + 1) * hsize].astype(jnp.bfloat16)

    for m, out in enumerate((o0, o1, o2, o3)):
        out[0] = slot_ref[chip ^ m]

    @pl.when(step == 1)
    def _():
        for h in range(CHIPS):
            key_ref[:, h * hsize : (h + 1) * hsize] = slot_ref[h]

    @pl.when(step == 2)
    def _():
        for h in range(CHIPS):
            val_ref[:, h * hsize : (h + 1) * hsize] = slot_ref[h]


def project(where, raw, gain, cosine, sine, weights):
    rows, wide = raw[0].shape
    hsize = cosine.shape[1]
    whole = lambda a: pl.BlockSpec(a.shape, lambda j, s: (0,) * a.ndim)
    cols = weights[0].shape[1] // 3
    return pl.pallas_call(
        project_kernel,
        grid_spec=pltpu.PrefetchScalarGridSpec(
            num_scalar_prefetch=1,
            grid=(3,),
            in_specs=[whole(a) for a in (*raw, gain, cosine, sine)]
            + [pl.BlockSpec((w.shape[0], cols), lambda j, s: (0, j)) for w in weights],
            out_specs=[pl.BlockSpec((1, rows, hsize), lambda j, s: (j, 0, 0))] * CHIPS
            + [pl.BlockSpec((rows, cols), lambda j, s: (0, 0))] * 2,
            scratch_shapes=[
                pltpu.VMEM((2 * LINE, rows, wide // 2), jnp.bfloat16),
                pltpu.VMEM((CHIPS, rows, hsize), jnp.bfloat16),
            ],
        ),
        out_shape=[jax.ShapeDtypeStruct((3, rows, hsize), jnp.bfloat16)] * CHIPS
        + [jax.ShapeDtypeStruct((rows, cols), jnp.bfloat16)] * 2,
        compiler_params=pltpu.CompilerParams(vmem_limit_bytes=48 << 20),
        name="project",
    )(where, *raw, gain, cosine, sine, *weights)


def attend_kernel(
    where_ref, start_ref, low_ref, a0, a1, a2, a3, b0, b1, b2, b3, o0, o1, o2, o3,
    keys, vals, sem, *, scale,
):
    chip, core = where_ref[0], where_ref[1]
    rows, hsize = a0.shape[1], a0.shape[2]
    copies = []
    for part, refs in ((0, (a0, a1, a2, a3)), (1, (b0, b1, b2, b3))):
        for m, ref in enumerate(refs):
            block = 2 * (chip ^ m) + (core if part == 0 else 1 - core)
            keys[block] = ref[1]
            vals[block] = ref[2]
    docs = start_ref.shape[0]
    for m, (ref, out) in enumerate(((a0, o0), (a1, o1), (a2, o2), (a3, o3))):
        block = 2 * (chip ^ m) + core
        query = ref[0]
        qpos = block * rows + lax.broadcasted_iota(jnp.int32, (rows, 1), 0)
        begin = jnp.zeros((rows, 1), jnp.int32)
        for d in range(docs):
            begin = jnp.where(start_ref[d] <= qpos, start_ref[d], begin)

        def tile(number, state, block=block, query=query, qpos=qpos, begin=begin):
            running, totals, accum = state
            kv = block - number
            kpos = kv * rows + lax.broadcasted_iota(jnp.int32, (1, rows), 1)
            score = scale * lax.dot_general(
                query, keys[kv], (((1,), (1,)), ((), ())), preferred_element_type=jnp.float32
            )
            keep = (kpos >= begin) & (kpos <= qpos)
            score = jnp.where(keep, score, -1e30)
            newmax = jnp.maximum(running, jnp.max(score, axis=1, keepdims=True))
            weight = jnp.exp(score - newmax)
            factor = jnp.exp(running - newmax)
            totals = totals * factor + jnp.sum(weight, axis=1, keepdims=True)
            accum = accum * factor + jnp.dot(
                weight.astype(jnp.bfloat16), vals[kv], preferred_element_type=jnp.float32
            )
            return newmax, totals, accum

        state = (
            jnp.full((rows, 1), -1e30, jnp.float32),
            jnp.zeros((rows, 1), jnp.float32),
            jnp.zeros((rows, hsize), jnp.float32),
        )
        running, totals, accum = lax.fori_loop(0, block - low_ref[block] + 1, tile, state)
        out[...] = (accum / totals).astype(jnp.bfloat16)


def attend(where, starts, low, own, sibling, scale):
    rows, hsize = own[0].shape[1:]
    smem = pl.BlockSpec(memory_space=pltpu.SMEM)
    return pl.pallas_call(
        functools.partial(attend_kernel, scale=scale),
        in_specs=[smem] * 3 + [vmem()] * (2 * CHIPS),
        out_specs=[vmem()] * CHIPS,
        out_shape=[jax.ShapeDtypeStruct((rows, hsize), jnp.bfloat16)] * CHIPS,
        scratch_shapes=[
            pltpu.VMEM((2 * CHIPS, rows, hsize), jnp.bfloat16),
            pltpu.VMEM((2 * CHIPS, rows, hsize), jnp.bfloat16),
            pltpu.SemaphoreType.DMA,
        ],
        compiler_params=pltpu.CompilerParams(vmem_limit_bytes=48 << 20),
        name="attend",
    )(where, starts, low, *own, *sibling)


def mix_kernel(where_ref, own, u1, u2, u3, d1, d2, d3, w_ref, out_ref):
    line = where_ref[2]
    blocks = [
        own[...],
        jnp.where(line >= 1, u1[...], d3[...]),
        jnp.where(line >= 2, u2[...], d2[...]),
        jnp.where(line >= 3, u3[...], d1[...]),
    ]
    total = None
    for d in range(LINE):
        part = jnp.dot(blocks[d], w_ref[(line - d) & 3], preferred_element_type=jnp.float32)
        total = part if total is None else total + part
    out_ref[...] = total.astype(jnp.bfloat16)


def mix(where, raw, w_all):
    return pl.pallas_call(
        mix_kernel,
        in_specs=[pl.BlockSpec(memory_space=pltpu.SMEM)] + [vmem()] * 8,
        out_specs=vmem(),
        out_shape=jax.ShapeDtypeStruct((raw[0].shape[0], w_all.shape[2]), jnp.bfloat16),
        compiler_params=pltpu.CompilerParams(vmem_limit_bytes=48 << 20),
        name="mix",
    )(where, *raw, w_all)


def blocks_plan(tokens, gain, w_qkv, w_out, lengths):
    rows, wide = tokens.shape
    depth, _, heads, hsize = w_qkv.shape
    mine = lax.axis_index("gx")
    line = lax.axis_index("gy")
    chip, core = mine // 2, mine % 2
    where = jnp.stack([chip, core, line]).astype(jnp.int32)

    ups, downs = along_line(tokens)

    flat = w_qkv.reshape(depth, 3 * heads * hsize)
    across, along = swap(flat, 2), swap(flat, 4)
    half = depth // 2
    far = (swap(along[:half], 2), swap(across[half:], 4))
    held = (flat, across, along, *far)
    weights = held + tuple(swap(w, 1) for w in held)

    glob = mine * rows + jnp.arange(rows, dtype=jnp.int32)
    cosine, sine = tables(glob - begins(lengths, glob), hsize)
    cosine = jnp.concatenate([cosine, cosine], axis=1)
    sine = jnp.concatenate([-sine, sine], axis=1)
    starts = (jnp.cumsum(lengths) - lengths).astype(jnp.int32)
    firsts = jnp.arange(2 * CHIPS, dtype=jnp.int32) * rows
    low = (begins(lengths, firsts) // rows).astype(jnp.int32)

    *sent, keys, vals = project(
        where, (tokens, *ups, *downs), gain.reshape(LINE, 1, wide), cosine, sine, weights
    )
    own = [sent[0]] + [swap(sent[m], 2 * m) for m in range(1, CHIPS)]
    sibling = [swap(a, 1) for a in own]
    heads_out = attend(where, starts, low, own, sibling, 1.0 / math.sqrt(hsize))
    back = [heads_out[0]] + [swap(heads_out[m], 2 * m) for m in range(1, CHIPS)]

    odd, high = (chip & 1) == 1, (chip & 2) == 2
    pairs = []
    for a, b in ((back[0], back[1]), (back[2], back[3])):
        pairs.append(jnp.concatenate([jnp.where(odd, b, a), jnp.where(odd, a, b)], axis=1))
    attended = jnp.concatenate(
        [jnp.where(high, pairs[1], pairs[0]), jnp.where(high, pairs[0], pairs[1])], axis=1
    )
    w_late, attended = lax.optimization_barrier((w_out, attended))
    w_all = lax.all_gather(w_late, "gx", axis=0, tiled=True)
    ups, downs = along_line(attended)
    mixed = mix(where, (attended, *ups, *downs), w_all.reshape(LINE, wide, w_out.shape[1]))
    return (mixed, keys.reshape(rows, heads, hsize), vals.reshape(rows, heads, hsize))


def local(sizes, tokens, gain, w_qkv, w_out, lengths):
    heads = w_qkv.shape[2]
    fits = sizes == (2 * CHIPS, LINE) and heads == CHIPS and tokens.shape[1] == 2 * w_qkv.shape[0]
    plan = blocks_plan if fits else general
    return plan(tokens, gain, w_qkv, w_out, lengths)


def solution(mesh):
    sizes = (mesh.shape["gx"], mesh.shape["gy"])
    return jax.shard_map(
        functools.partial(local, sizes),
        mesh=mesh,
        in_specs=(P("gx", "gy"), P(), P("gx", None, "gy", None), P("gx", "gy"), P()),
        out_specs=(P("gx", "gy"), P("gx", "gy", None), P("gx", "gy", None)),
        check_vma=False,
    )
```

```python
import functools
import math

import jax
import jax.numpy as jnp
from jax import lax
from jax.experimental import pallas as pl
from jax.experimental.pallas import tpu as pltpu
from jax.sharding import PartitionSpec as P


def tables(position, hsize):
    half = hsize // 2
    freq = 10000.0 ** (-(2.0 * jnp.arange(half, dtype=jnp.float32)) / hsize)
    angle = position.astype(jnp.float32)[:, None] * freq[None, :]
    return jnp.cos(angle), jnp.sin(angle)


def rotate(vectors, position):
    half = vectors.shape[-1] // 2
    cosine, sine = tables(position, vectors.shape[-1])
    cosine, sine = cosine[:, None, :], sine[:, None, :]
    first = vectors[..., :half]
    second = vectors[..., half:]
    return jnp.concatenate(
        [first * cosine - second * sine, second * cosine + first * sine], axis=-1
    )


def begins(lengths, glob):
    doc_start = jnp.cumsum(lengths) - lengths
    return jnp.max(jnp.where(doc_start[None, :] <= glob[:, None], doc_start[None, :], 0), axis=1)


def block_rows(count):
    size = count
    while size > 1024 and size % 2 == 0:
        size = size // 2
    return size


def general(tokens, gain, w_qkv, w_out, lengths):
    tok_dev = tokens.shape[0]
    hloc = w_qkv.shape[2]
    hsize = w_qkv.shape[3]
    whole = lax.all_gather(tokens, "gy", axis=1, tiled=True)
    wide = whole.astype(jnp.float32)
    meansq = jnp.mean(wide * wide, axis=-1, keepdims=True)
    normed = (wide * lax.rsqrt(meansq + 1e-06) * gain[None, :]).astype(jnp.bfloat16)
    piece = lax.all_gather(w_qkv, "gx", axis=0, tiled=True)
    projected = jnp.dot(
        normed, piece.reshape(piece.shape[0], -1), preferred_element_type=jnp.float32
    )
    projected = projected.reshape(tok_dev, 3, hloc, hsize)
    mine = lax.axis_index("gx")
    glob = mine * tok_dev + jnp.arange(tok_dev, dtype=jnp.int32)
    begin = begins(lengths, glob)
    position = glob - begin
    query = rotate(projected[:, 0], position).astype(jnp.bfloat16)
    keys_own = rotate(projected[:, 1], position).astype(jnp.bfloat16)
    vals_own = projected[:, 2].astype(jnp.bfloat16)
    scale = 1.0 / math.sqrt(hsize)
    initial = (
        jnp.full((hloc, tok_dev), -1e30, jnp.float32),
        jnp.zeros((hloc, tok_dev), jnp.float32),
        jnp.zeros((hloc, tok_dev, hsize), jnp.float32),
    )
    keys_piece = lax.all_gather(keys_own, "gx", axis=0, tiled=True)
    vals_piece = lax.all_gather(vals_own, "gx", axis=0, tiled=True)
    count = keys_piece.shape[0]
    size = block_rows(count)

    def one_tile(number, state):
        running, totals, accum = state
        first = (number * size).astype(jnp.int32)
        keys_blk = lax.dynamic_slice_in_dim(keys_piece, first, size, 0)
        vals_blk = lax.dynamic_slice_in_dim(vals_piece, first, size, 0)
        kidx = first + jnp.arange(size, dtype=jnp.int32)
        score = (
            jnp.einsum("qhd,khd->hqk", query, keys_blk, preferred_element_type=jnp.float32) * scale
        )
        keep = (kidx[None, :] >= begin[:, None]) & (kidx[None, :] <= glob[:, None])
        score = jnp.where(keep[None], score, -1e30)
        newmax = jnp.maximum(running, jnp.max(score, axis=-1))
        weight = jnp.where(keep[None], jnp.exp(score - newmax[..., None]), 0.0)
        factor = jnp.exp(running - newmax)
        totals = totals * factor + jnp.sum(weight, axis=-1)
        update = jnp.einsum(
            "hqk,khd->hqd",
            weight.astype(jnp.bfloat16),
            vals_blk,
            preferred_element_type=jnp.float32,
        )
        accum = accum * factor[..., None] + update
        return (newmax, totals, accum)

    running, totals, accum = lax.fori_loop(0, count // size, one_tile, initial)
    attended = (accum / totals[..., None]).astype(jnp.bfloat16)
    attended = jnp.transpose(attended, (1, 0, 2)).reshape(tok_dev, hloc * hsize)
    all_heads = lax.all_gather(attended, "gy", axis=1, tiled=True)
    mixed = jnp.dot(
        all_heads, lax.all_gather(w_out, "gx", axis=0, tiled=True),
        preferred_element_type=jnp.float32,
    ).astype(jnp.bfloat16)
    return (mixed, keys_own, vals_own)


LINE = 4
CHIPS = 4
NORM_EFFORT = 8 << 30
EARLY_EFFORT = 16 << 30


def swap(x, mask):
    return lax.ppermute(x, "gx", [(i, i ^ mask) for i in range(2 * CHIPS)])


def outer(x):
    return lax.ppermute(x, "gy", [(0, 1), (1, 0), (2, 3), (3, 2)])


def inner(x):
    return lax.ppermute(x, "gy", [(1, 2), (2, 1)])


def outward(x):
    return lax.ppermute(x, "gy", [(1, 0), (2, 3)])


def order(line):
    low = line < 2
    return line ^ 1, jnp.where(low, 2, 1), jnp.where(low, 3, 0), (line == 0) | (line == LINE - 1)


def vmem():
    return pl.BlockSpec(memory_space=pltpu.VMEM)


def smem():
    return pl.BlockSpec(memory_space=pltpu.SMEM)


def hbm():
    return pl.BlockSpec(memory_space=pl.ANY)


def full(array):
    return pl.BlockSpec(array.shape, lambda *_: (0,) * array.ndim)


def effort(flops):
    return pl.CostEstimate(flops=flops, transcendentals=0, bytes_accessed=8 << 20)


def normalize_kernel(where_ref, own, near, q1, p2, q2, p3, gain_ref, x_ref):
    line = where_ref[2]
    wide = own.shape[1]
    second, third, fourth, end = order(line)
    raw = [
        own[...].astype(jnp.float32),
        near[...].astype(jnp.float32),
        jnp.where(end, p2[...], q1[...]).astype(jnp.float32),
        jnp.where(end, p3[...], q2[...]).astype(jnp.float32),
    ]
    square = sum(jnp.sum(r * r, axis=1, keepdims=True) for r in raw)
    scale = lax.rsqrt(square * (1.0 / (LINE * wide)) + 1e-06)
    for r, feature in zip(raw, (line, second, third, fourth)):
        normed = (r * scale * gain_ref[feature]).astype(jnp.bfloat16)
        x_ref[2 * feature] = normed[:, : wide // 2]
        x_ref[2 * feature + 1] = normed[:, wide // 2 :]


def normalize(where, blocks, gain):
    rows, wide = blocks[0].shape
    return pl.pallas_call(
        normalize_kernel,
        in_specs=[smem()] + [vmem()] * 7,
        out_specs=vmem(),
        out_shape=jax.ShapeDtypeStruct((2 * LINE, rows, wide // 2), jnp.bfloat16),
        compiler_params=pltpu.CompilerParams(vmem_limit_bytes=20 << 20),
        cost_estimate=effort(NORM_EFFORT),
        name="normalize",
    )(where, *blocks, gain)


def project_kernel(where_ref, x_ref, cos_ref, sin_ref, *refs):
    weights, outs, (slot_ref,) = refs[:10], refs[10:16], refs[16:]
    sent, key_ref, val_ref = outs[:CHIPS], outs[CHIPS], outs[CHIPS + 1]
    step = pl.program_id(0)
    chip, core = where_ref[0], where_ref[1]
    wide = 2 * x_ref.shape[2]
    hsize = cos_ref.shape[1]

    total = None
    for side in range(2):
        half = core if side == 0 else 1 - core
        for m in range(CHIPS):
            x = x_ref[2 * (chip ^ m) + half]
            if m < 3:
                parts = [(x, weights[5 * side + m])]
            else:
                parts = [
                    (x[:, : wide // 4], weights[5 * side + 3]),
                    (x[:, wide // 4 :], weights[5 * side + 4]),
                ]
            for left, right in parts:
                part = jnp.dot(left, right[...], preferred_element_type=jnp.float32)
                total = part if total is None else total + part

    @pl.when(step < 2)
    def _():
        for h in range(CHIPS):
            u = total[:, h * hsize : (h + 1) * hsize]
            u = u * cos_ref[...] + pltpu.roll(u, hsize // 2, 1) * sin_ref[...]
            slot_ref[h] = u.astype(jnp.bfloat16)

    @pl.when(step == 2)
    def _():
        for h in range(CHIPS):
            slot_ref[h] = total[:, h * hsize : (h + 1) * hsize].astype(jnp.bfloat16)

    for m in range(CHIPS):
        sent[m][0] = slot_ref[chip ^ m]

    @pl.when(step == 1)
    def _():
        for h in range(CHIPS):
            key_ref[:, h * hsize : (h + 1) * hsize] = slot_ref[h]

    @pl.when(step == 2)
    def _():
        for h in range(CHIPS):
            val_ref[:, h * hsize : (h + 1) * hsize] = slot_ref[h]


def project(where, x, cosine, sine, weights):
    rows, hsize = cosine.shape
    wide = 2 * x.shape[2]
    cols = weights[0].shape[1] // 3
    return pl.pallas_call(
        project_kernel,
        grid=(3,),
        in_specs=[smem()]
        + [full(a) for a in (x, cosine, sine)]
        + [pl.BlockSpec((w.shape[0], cols), lambda j: (0, j)) for w in weights],
        out_specs=[pl.BlockSpec((1, rows, hsize), lambda j: (j, 0, 0))] * CHIPS
        + [pl.BlockSpec((rows, cols), lambda j: (0, 0))] * 2,
        out_shape=[jax.ShapeDtypeStruct((3, rows, hsize), jnp.bfloat16)] * CHIPS
        + [jax.ShapeDtypeStruct((rows, cols), jnp.bfloat16)] * 2,
        scratch_shapes=[
            pltpu.VMEM((CHIPS, rows, hsize), jnp.bfloat16),
        ],
        compiler_params=pltpu.CompilerParams(vmem_limit_bytes=24 << 20),
        cost_estimate=effort(2 * rows * LINE * wide * 3 * cols),
        name="project",
    )(where, x, cosine, sine, *weights)


def attend_kernel(where_ref, start_ref, *refs, scale):
    pieces, outs, (keys, vals) = refs[:8], refs[8:12], refs[12:]
    chip, core = where_ref[0], where_ref[1]
    _, rows, hsize = pieces[0].shape
    for side in range(2):
        for n in range(CHIPS):
            block = 2 * (chip ^ n) + (core if side == 0 else 1 - core)
            keys[block] = pieces[CHIPS * side + n][1]
            vals[block] = pieces[CHIPS * side + n][2]
    for m in range(CHIPS):
        block = 2 * (chip ^ m) + core
        query = pieces[m][0]
        qpos = block * rows + lax.broadcasted_iota(jnp.int32, (rows, 1), 0)
        begin = jnp.zeros((rows, 1), jnp.int32)
        lowest = jnp.int32(0)
        for d in range(start_ref.shape[0]):
            begin = jnp.where(start_ref[d] <= qpos, start_ref[d], begin)
            lowest = jnp.where(start_ref[d] <= block * rows, start_ref[d], lowest)

        def tile(number, state, block=block, query=query, qpos=qpos, begin=begin):
            running, totals, accum = state
            kv = block - number
            kpos = kv * rows + lax.broadcasted_iota(jnp.int32, (1, rows), 1)
            score = scale * lax.dot_general(
                query, keys[kv], (((1,), (1,)), ((), ())), preferred_element_type=jnp.float32
            )
            keep = (kpos >= begin) & (kpos <= qpos)
            score = jnp.where(keep, score, -1e30)
            newmax = jnp.maximum(running, jnp.max(score, axis=1, keepdims=True))
            weight = jnp.exp(score - newmax)
            factor = jnp.exp(running - newmax)
            totals = totals * factor + jnp.sum(weight, axis=1, keepdims=True)
            accum = accum * factor + jnp.dot(
                weight.astype(jnp.bfloat16), vals[kv], preferred_element_type=jnp.float32
            )
            return newmax, totals, accum

        state = (
            jnp.full((rows, 1), -1e30, jnp.float32),
            jnp.zeros((rows, 1), jnp.float32),
            jnp.zeros((rows, hsize), jnp.float32),
        )
        running, totals, accum = lax.fori_loop(0, block - lax.div(lowest, rows) + 1, tile, state)
        outs[m][...] = (accum / totals).astype(jnp.bfloat16)


def attend(where, starts, pieces, scale):
    _, rows, hsize = pieces[0].shape
    return pl.pallas_call(
        functools.partial(attend_kernel, scale=scale),
        in_specs=[smem()] * 2 + [vmem()] * len(pieces),
        out_specs=[vmem()] * CHIPS,
        out_shape=[jax.ShapeDtypeStruct((rows, hsize), jnp.bfloat16)] * CHIPS,
        scratch_shapes=[pltpu.VMEM((2 * CHIPS, rows, hsize), jnp.bfloat16)] * 2,
        compiler_params=pltpu.CompilerParams(vmem_limit_bytes=16 << 20),
        cost_estimate=effort(16 * 2 * rows * LINE * rows * hsize),
        name="attend",
    )(where, starts, *pieces)


def early_kernel(where_ref, own, near, q1, p2, *refs):
    pieces, total_ref, last_ref, w_ref = refs[:10], refs[10], refs[11], refs[12]
    chip, core, line = where_ref[0], where_ref[1], where_ref[2]
    depth = pieces[0].shape[0]
    for side in range(2):
        for m in range(CHIPS):
            block = 2 * (chip ^ m) + (core if side == 0 else 1 - core)
            if m < 3:
                w_ref[block] = pieces[5 * side + m][...]
            else:
                w_ref[block, : depth // 2] = pieces[5 * side + 3][...]
                w_ref[block, depth // 2 :] = pieces[5 * side + 4][...]

    def term(block, feature):
        return jnp.dot(
            block[:, :depth], w_ref[2 * feature], preferred_element_type=jnp.float32
        ) + jnp.dot(block[:, depth:], w_ref[2 * feature + 1], preferred_element_type=jnp.float32)

    second, third, fourth, end = order(line)
    total = term(own[...], line) + term(near[...], second)
    total_ref[...] = total + term(jnp.where(end, p2[...], q1[...]), third)
    last_ref[:depth] = w_ref[2 * fourth]
    last_ref[depth:] = w_ref[2 * fourth + 1]


def early(where, blocks, pieces):
    rows, wide = blocks[0].shape
    depth, cols = pieces[0].shape
    return pl.pallas_call(
        early_kernel,
        in_specs=[smem()] + [vmem()] * (len(blocks) + len(pieces)),
        out_specs=[vmem()] * 2,
        out_shape=[
            jax.ShapeDtypeStruct((rows, cols), jnp.float32),
            jax.ShapeDtypeStruct((wide, cols), jnp.bfloat16),
        ],
        scratch_shapes=[pltpu.VMEM((2 * CHIPS, depth, cols), jnp.bfloat16)],
        compiler_params=pltpu.CompilerParams(vmem_limit_bytes=16 << 20),
        cost_estimate=effort(EARLY_EFFORT),
        name="early",
    )(where, *blocks, *pieces)


def last_kernel(where_ref, q2, p3, total_ref, w_ref, out_ref):
    end = order(where_ref[2])[3]
    block = jnp.where(end, p3[...], q2[...])
    total = total_ref[...] + jnp.dot(block, w_ref[...], preferred_element_type=jnp.float32)
    out_ref[...] = total.astype(jnp.bfloat16)


def last(where, q2, p3, total, w_last):
    return pl.pallas_call(
        last_kernel,
        in_specs=[smem()] + [vmem()] * 4,
        out_specs=vmem(),
        out_shape=jax.ShapeDtypeStruct(total.shape, jnp.bfloat16),
        compiler_params=pltpu.CompilerParams(vmem_limit_bytes=8 << 20),
        cost_estimate=effort(2 * total.shape[0] * w_last.size),
        name="last",
    )(where, q2, p3, total, w_last)


def heads_in_order(back, chip):
    odd, high = (chip & 1) == 1, (chip & 2) == 2
    low, top = [
        jnp.concatenate([jnp.where(odd, b, a), jnp.where(odd, a, b)], axis=1)
        for a, b in (back[:2], back[2:])
    ]
    return jnp.concatenate([jnp.where(high, top, low), jnp.where(high, low, top)], axis=1)


def together(*arrays):
    return lax.optimization_barrier(arrays)


def blocks_plan(tokens, gain, w_qkv, w_out, lengths):
    rows, wide = tokens.shape
    depth, _, heads, hsize = w_qkv.shape
    half = depth // 2
    mine = lax.axis_index("gx")
    line = lax.axis_index("gy")
    chip, core = mine // 2, mine % 2
    where = jnp.stack([chip, core, line]).astype(jnp.int32)
    starts = (jnp.cumsum(lengths) - lengths).astype(jnp.int32)
    glob = mine * rows + jnp.arange(rows, dtype=jnp.int32)
    cosine, sine = tables(glob - begins(lengths, glob), hsize)
    cosine = jnp.concatenate([cosine, cosine], axis=1)
    sine = jnp.concatenate([-sine, sine], axis=1)

    flat = w_qkv.reshape(depth, -1)
    near, q1 = outer(tokens), inner(tokens)
    q2, p2 = inner(near), outward(q1)
    w_x, w_y = swap(flat, 2), swap(flat, 4)
    q2, p2, w_x, w_y = together(q2, p2, w_x, w_y)
    p3, far_a, far_b = outward(q2), swap(w_y[:half], 2), swap(w_x[half:], 4)
    held = (flat, w_x, w_y, far_a, far_b)
    weights = held + tuple(swap(w, 1) for w in held)
    x = normalize(where, (tokens, near, q1, p2, q2, p3), gain.reshape(LINE, 1, wide))
    *sent, keys, vals = project(where, x, cosine, sine, weights)

    pieces = [sent[0]] + [swap(sent[m], 2 * m) for m in range(1, CHIPS)]
    *pieces, w_late = together(*pieces, w_out)
    w_x, w_y = swap(w_late, 2), swap(w_late, 4)
    heads_out = attend(
        where, starts, pieces + [swap(a, 1) for a in pieces], 1.0 / math.sqrt(hsize)
    )
    *heads_out, w_x, w_y = together(*heads_out, w_x, w_y)
    back = [heads_out[0]] + [swap(heads_out[m], 2 * m) for m in range(1, CHIPS)]
    attended = heads_in_order(back, chip)
    attended, w_x, w_y = together(attended, w_x, w_y)
    near, q1, far_a, far_b = together(
        outer(attended), inner(attended), swap(w_y[:half], 2), swap(w_x[half:], 4)
    )
    pieces = (w_late, w_x, w_y, far_a, far_b)
    q2, p2 = inner(near), outward(q1)
    q2, *others = together(q2, *[swap(w, 1) for w in pieces])
    p3 = outward(q2)
    total, w_last = early(where, (attended, near, q1, p2), (*pieces, *others))
    mixed = last(where, q2, p3, total, w_last)
    return (mixed, keys.reshape(rows, heads, hsize), vals.reshape(rows, heads, hsize))


def local(sizes, tokens, gain, w_qkv, w_out, lengths):
    heads = w_qkv.shape[2]
    fits = sizes == (2 * CHIPS, LINE) and heads == CHIPS and tokens.shape[1] == 2 * w_qkv.shape[0]
    plan = blocks_plan if fits else general
    return plan(tokens, gain, w_qkv, w_out, lengths)


def solution(mesh):
    sizes = (mesh.shape["gx"], mesh.shape["gy"])
    return jax.shard_map(
        functools.partial(local, sizes),
        mesh=mesh,
        in_specs=(P("gx", "gy"), P(), P("gx", None, "gy", None), P("gx", "gy"), P()),
        out_specs=(P("gx", "gy"), P("gx", "gy", None), P("gx", "gy", None)),
        check_vma=False,
    )
```

```python
import functools
import math

import jax
import jax.numpy as jnp
from jax import lax
from jax.experimental import pallas as pl
from jax.experimental.pallas import tpu as pltpu
from jax.sharding import PartitionSpec as P


def tables(position, hsize):
    half = hsize // 2
    freq = 10000.0 ** (-(2.0 * jnp.arange(half, dtype=jnp.float32)) / hsize)
    angle = position.astype(jnp.float32)[:, None] * freq[None, :]
    return jnp.cos(angle), jnp.sin(angle)


def rotate(vectors, position):
    half = vectors.shape[-1] // 2
    cosine, sine = tables(position, vectors.shape[-1])
    cosine, sine = cosine[:, None, :], sine[:, None, :]
    first = vectors[..., :half]
    second = vectors[..., half:]
    return jnp.concatenate(
        [first * cosine - second * sine, second * cosine + first * sine], axis=-1
    )


def begins(lengths, glob):
    doc_start = jnp.cumsum(lengths) - lengths
    return jnp.max(jnp.where(doc_start[None, :] <= glob[:, None], doc_start[None, :], 0), axis=1)


def block_rows(count):
    size = count
    while size > 1024 and size % 2 == 0:
        size = size // 2
    return size


def general(tokens, gain, w_qkv, w_out, lengths):
    tok_dev = tokens.shape[0]
    hloc = w_qkv.shape[2]
    hsize = w_qkv.shape[3]
    whole = lax.all_gather(tokens, "gy", axis=1, tiled=True)
    wide = whole.astype(jnp.float32)
    meansq = jnp.mean(wide * wide, axis=-1, keepdims=True)
    normed = (wide * lax.rsqrt(meansq + 1e-06) * gain[None, :]).astype(jnp.bfloat16)
    piece = lax.all_gather(w_qkv, "gx", axis=0, tiled=True)
    projected = jnp.dot(
        normed, piece.reshape(piece.shape[0], -1), preferred_element_type=jnp.float32
    )
    projected = projected.reshape(tok_dev, 3, hloc, hsize)
    mine = lax.axis_index("gx")
    glob = mine * tok_dev + jnp.arange(tok_dev, dtype=jnp.int32)
    begin = begins(lengths, glob)
    position = glob - begin
    query = rotate(projected[:, 0], position).astype(jnp.bfloat16)
    keys_own = rotate(projected[:, 1], position).astype(jnp.bfloat16)
    vals_own = projected[:, 2].astype(jnp.bfloat16)
    scale = 1.0 / math.sqrt(hsize)
    initial = (
        jnp.full((hloc, tok_dev), -1e30, jnp.float32),
        jnp.zeros((hloc, tok_dev), jnp.float32),
        jnp.zeros((hloc, tok_dev, hsize), jnp.float32),
    )
    keys_piece = lax.all_gather(keys_own, "gx", axis=0, tiled=True)
    vals_piece = lax.all_gather(vals_own, "gx", axis=0, tiled=True)
    count = keys_piece.shape[0]
    size = block_rows(count)

    def one_tile(number, state):
        running, totals, accum = state
        first = (number * size).astype(jnp.int32)
        keys_blk = lax.dynamic_slice_in_dim(keys_piece, first, size, 0)
        vals_blk = lax.dynamic_slice_in_dim(vals_piece, first, size, 0)
        kidx = first + jnp.arange(size, dtype=jnp.int32)
        score = (
            jnp.einsum("qhd,khd->hqk", query, keys_blk, preferred_element_type=jnp.float32) * scale
        )
        keep = (kidx[None, :] >= begin[:, None]) & (kidx[None, :] <= glob[:, None])
        score = jnp.where(keep[None], score, -1e30)
        newmax = jnp.maximum(running, jnp.max(score, axis=-1))
        weight = jnp.where(keep[None], jnp.exp(score - newmax[..., None]), 0.0)
        factor = jnp.exp(running - newmax)
        totals = totals * factor + jnp.sum(weight, axis=-1)
        update = jnp.einsum(
            "hqk,khd->hqd",
            weight.astype(jnp.bfloat16),
            vals_blk,
            preferred_element_type=jnp.float32,
        )
        accum = accum * factor[..., None] + update
        return (newmax, totals, accum)

    running, totals, accum = lax.fori_loop(0, count // size, one_tile, initial)
    attended = (accum / totals[..., None]).astype(jnp.bfloat16)
    attended = jnp.transpose(attended, (1, 0, 2)).reshape(tok_dev, hloc * hsize)
    all_heads = lax.all_gather(attended, "gy", axis=1, tiled=True)
    mixed = jnp.dot(
        all_heads, lax.all_gather(w_out, "gx", axis=0, tiled=True),
        preferred_element_type=jnp.float32,
    ).astype(jnp.bfloat16)
    return (mixed, keys_own, vals_own)


LINE = 4
CHIPS = 4
NORM_EFFORT = 8 << 30
PAIRS = ((1, 2), (3, 0))
EARLY_EFFORT = 16 << 30


def swap(x, mask):
    return lax.ppermute(x, "gx", [(i, i ^ mask) for i in range(2 * CHIPS)])


def outer(x):
    return lax.ppermute(x, "gy", [(0, 1), (1, 0), (2, 3), (3, 2)])


def inner(x):
    return lax.ppermute(x, "gy", [(1, 2), (2, 1)])


def outward(x):
    return lax.ppermute(x, "gy", [(1, 0), (2, 3)])


def order(line):
    low = line < 2
    return line ^ 1, jnp.where(low, 2, 1), jnp.where(low, 3, 0), (line == 0) | (line == LINE - 1)


def vmem():
    return pl.BlockSpec(memory_space=pltpu.VMEM)


def smem():
    return pl.BlockSpec(memory_space=pltpu.SMEM)


def hbm():
    return pl.BlockSpec(memory_space=pltpu.HBM)


def full(array):
    return pl.BlockSpec(array.shape, lambda *_: (0,) * array.ndim)


def effort(flops):
    return pl.CostEstimate(flops=flops, transcendentals=0, bytes_accessed=8 << 20)


def halves_kernel(x_ref, y_ref, upper_ref, lower_ref):
    upper_ref[...] = y_ref[...]
    lower_ref[...] = x_ref[...]


def halves(across, along):
    rows, cols = across.shape[0] // 2, across.shape[1]
    block = lambda half: pl.BlockSpec((rows, cols), lambda _: (half, 0))
    return pl.pallas_call(
        halves_kernel,
        grid=(1,),
        in_specs=[block(1), block(0)],
        out_specs=[block(0)] * 2,
        out_shape=[jax.ShapeDtypeStruct((rows, cols), across.dtype)] * 2,
        compiler_params=pltpu.CompilerParams(vmem_limit_bytes=6 << 20),
        name="halves",
    )(across, along)


def normalize_kernel(where_ref, *refs):
    blocks, (gain_ref, x_ref, raw_ref, sems) = refs[:6], refs[6:]
    chip, line = where_ref[0], where_ref[2]
    wide = raw_ref.shape[2]
    copies = [
        pltpu.make_async_copy(block, raw_ref.at[n], sems.at[n]) for n, block in enumerate(blocks)
    ]
    for copy in copies:
        copy.start()
    for copy in copies:
        copy.wait()
    own, near, q1, p2, q2, p3 = [raw_ref[n] for n in range(6)]
    second, third, fourth, end = order(line)
    raw = [
        own.astype(jnp.float32),
        near.astype(jnp.float32),
        jnp.where(end, p2, q1).astype(jnp.float32),
        jnp.where(end, p3, q2).astype(jnp.float32),
    ]
    square = sum(jnp.sum(r * r, axis=1, keepdims=True) for r in raw)
    scale = lax.rsqrt(square * (1.0 / (LINE * wide)) + 1e-06)
    for r, feature in zip(raw, (line, second, third, fourth)):
        normed = (r * scale * gain_ref[feature]).astype(jnp.bfloat16)
        x_ref[:, pl.ds(pl.multiple_of((feature ^ chip) * wide, wide), wide)] = normed


def normalize(where, blocks, gain):
    rows, wide = blocks[0].shape
    return pl.pallas_call(
        normalize_kernel,
        in_specs=[smem()] + [hbm()] * 6 + [vmem()],
        out_specs=vmem(),
        out_shape=jax.ShapeDtypeStruct((rows, LINE * wide), jnp.bfloat16),
        scratch_shapes=[pltpu.VMEM((6, rows, wide), jnp.bfloat16), pltpu.SemaphoreType.DMA((6,))],
        compiler_params=pltpu.CompilerParams(vmem_limit_bytes=12 << 20),
        cost_estimate=effort(NORM_EFFORT),
        name="normalize",
    )(where, *blocks, gain)


def head_columns(chip, pair, hsize):
    for i, m in enumerate(pair):
        for j in range(3):
            source = pl.multiple_of((CHIPS * j + (chip ^ m)) * hsize, hsize)
            yield pl.ds(source, hsize), slice((3 * i + j) * hsize, (3 * i + j + 1) * hsize)


def project_kernel(where_ref, x_ref, cos_ref, sin_ref, *refs, pair):
    weights, (out_a, out_b, w_ref) = refs[:10], refs[10:]
    chip, core = where_ref[0], where_ref[1]
    hsize = cos_ref.shape[1]
    depth = weights[0].shape[0]
    for source, target in head_columns(chip, pair, hsize):
        for side, half in ((0, core), (1, 1 - core)):
            for m in range(5):
                piece = weights[5 * side + m]
                row = (2 * min(m, 3) + half) * depth + (depth // 2 if m == 4 else 0)
                row = pl.multiple_of(row, depth // 2)
                w_ref[pl.ds(row, piece.shape[0]), target] = piece[:, source]
    total = jnp.dot(x_ref[...], w_ref[...], preferred_element_type=jnp.float32)
    for i, out in enumerate((out_a, out_b)):
        for j in range(3):
            u = total[:, (3 * i + j) * hsize : (3 * i + j + 1) * hsize]
            if j < 2:
                u = u * cos_ref[...] + pltpu.roll(u, hsize // 2, 1) * sin_ref[...]
            out[j] = u.astype(jnp.bfloat16)


def project(where, pair, x, cosine, sine, weights):
    rows, hsize = cosine.shape
    return pl.pallas_call(
        functools.partial(project_kernel, pair=pair),
        in_specs=[smem()] + [vmem()] * (3 + len(weights)),
        out_specs=[vmem()] * 2,
        out_shape=[jax.ShapeDtypeStruct((3, rows, hsize), jnp.bfloat16)] * 2,
        scratch_shapes=[pltpu.VMEM((x.shape[1], 6 * hsize), jnp.bfloat16)],
        compiler_params=pltpu.CompilerParams(vmem_limit_bytes=20 << 20),
        cost_estimate=effort(2 * x.size * 6 * hsize),
        name="project",
    )(where, x, cosine, sine, *weights)


def attend_kernel(where_ref, start_ref, *refs, scale):
    pieces, outs, (keys, vals) = refs[:8], refs[8:12], refs[12:]
    chip, core = where_ref[0], where_ref[1]
    _, rows, hsize = pieces[0].shape
    for side in range(2):
        for n in range(CHIPS):
            block = 2 * (chip ^ n) + (core if side == 0 else 1 - core)
            keys[block] = pieces[CHIPS * side + n][1]
            vals[block] = pieces[CHIPS * side + n][2]
    for m in range(CHIPS):
        block = 2 * (chip ^ m) + core
        query = pieces[m][0]
        qpos = block * rows + lax.broadcasted_iota(jnp.int32, (rows, 1), 0)
        begin = jnp.zeros((rows, 1), jnp.int32)
        lowest = jnp.int32(0)
        for d in range(start_ref.shape[0]):
            begin = jnp.where(start_ref[d] <= qpos, start_ref[d], begin)
            lowest = jnp.where(start_ref[d] <= block * rows, start_ref[d], lowest)

        def tile(number, state, block=block, query=query, qpos=qpos, begin=begin):
            running, totals, accum = state
            kv = block - number
            kpos = kv * rows + lax.broadcasted_iota(jnp.int32, (1, rows), 1)
            score = scale * lax.dot_general(
                query, keys[kv], (((1,), (1,)), ((), ())), preferred_element_type=jnp.float32
            )
            keep = (kpos >= begin) & (kpos <= qpos)
            score = jnp.where(keep, score, -1e30)
            newmax = jnp.maximum(running, jnp.max(score, axis=1, keepdims=True))
            weight = jnp.exp(score - newmax)
            factor = jnp.exp(running - newmax)
            totals = totals * factor + jnp.sum(weight, axis=1, keepdims=True)
            accum = accum * factor + jnp.dot(
                weight.astype(jnp.bfloat16), vals[kv], preferred_element_type=jnp.float32
            )
            return newmax, totals, accum

        state = (
            jnp.full((rows, 1), -1e30, jnp.float32),
            jnp.zeros((rows, 1), jnp.float32),
            jnp.zeros((rows, hsize), jnp.float32),
        )
        running, totals, accum = lax.fori_loop(0, block - lax.div(lowest, rows) + 1, tile, state)
        outs[m][...] = (accum / totals).astype(jnp.bfloat16)


def attend(where, starts, pieces, scale):
    _, rows, hsize = pieces[0].shape
    return pl.pallas_call(
        functools.partial(attend_kernel, scale=scale),
        in_specs=[smem()] * 2 + [vmem()] * len(pieces),
        out_specs=[vmem()] * CHIPS,
        out_shape=[jax.ShapeDtypeStruct((rows, hsize), jnp.bfloat16)] * CHIPS,
        scratch_shapes=[pltpu.VMEM((2 * CHIPS, rows, hsize), jnp.bfloat16)] * 2,
        compiler_params=pltpu.CompilerParams(vmem_limit_bytes=16 << 20),
        cost_estimate=effort(16 * 2 * rows * LINE * rows * hsize),
        name="attend",
    )(where, starts, *pieces)


def early_kernel(where_ref, own, near, q1, p2, *refs):
    pieces, total_ref, last_ref, w_ref = refs[:10], refs[10], refs[11], refs[12]
    chip, core, line = where_ref[0], where_ref[1], where_ref[2]
    depth = pieces[0].shape[0]
    for side in range(2):
        for m in range(CHIPS):
            block = 2 * (chip ^ m) + (core if side == 0 else 1 - core)
            if m < 3:
                w_ref[block] = pieces[5 * side + m][...]
            else:
                w_ref[block, : depth // 2] = pieces[5 * side + 3][...]
                w_ref[block, depth // 2 :] = pieces[5 * side + 4][...]

    def term(block, feature):
        return jnp.dot(
            block[:, :depth], w_ref[2 * feature], preferred_element_type=jnp.float32
        ) + jnp.dot(block[:, depth:], w_ref[2 * feature + 1], preferred_element_type=jnp.float32)

    second, third, fourth, end = order(line)
    total = term(own[...], line) + term(near[...], second)
    total_ref[...] = total + term(jnp.where(end, p2[...], q1[...]), third)
    last_ref[:depth] = w_ref[2 * fourth]
    last_ref[depth:] = w_ref[2 * fourth + 1]


def early(where, blocks, pieces):
    rows, wide = blocks[0].shape
    depth, cols = pieces[0].shape
    return pl.pallas_call(
        early_kernel,
        in_specs=[smem()] + [vmem()] * (len(blocks) + len(pieces)),
        out_specs=[vmem()] * 2,
        out_shape=[
            jax.ShapeDtypeStruct((rows, cols), jnp.float32),
            jax.ShapeDtypeStruct((wide, cols), jnp.bfloat16),
        ],
        scratch_shapes=[pltpu.VMEM((2 * CHIPS, depth, cols), jnp.bfloat16)],
        compiler_params=pltpu.CompilerParams(vmem_limit_bytes=16 << 20),
        cost_estimate=effort(EARLY_EFFORT),
        name="early",
    )(where, *blocks, *pieces)


def last_kernel(where_ref, q2, p3, total_ref, w_ref, out_ref):
    end = order(where_ref[2])[3]
    block = jnp.where(end, p3[...], q2[...])
    total = total_ref[...] + jnp.dot(block, w_ref[...], preferred_element_type=jnp.float32)
    out_ref[...] = total.astype(jnp.bfloat16)


def last(where, q2, p3, total, w_last):
    return pl.pallas_call(
        last_kernel,
        in_specs=[smem()] + [vmem()] * 4,
        out_specs=vmem(),
        out_shape=jax.ShapeDtypeStruct(total.shape, jnp.bfloat16),
        compiler_params=pltpu.CompilerParams(vmem_limit_bytes=8 << 20),
        cost_estimate=effort(2 * total.shape[0] * w_last.size),
        name="last",
    )(where, q2, p3, total, w_last)


def heads_in_order(back, chip):
    odd, high = (chip & 1) == 1, (chip & 2) == 2
    low, top = [
        jnp.concatenate([jnp.where(odd, b, a), jnp.where(odd, a, b)], axis=1)
        for a, b in (back[:2], back[2:])
    ]
    return jnp.concatenate([jnp.where(high, top, low), jnp.where(high, low, top)], axis=1)


def together(*arrays):
    return lax.optimization_barrier(arrays)


def blocks_plan(tokens, gain, w_qkv, w_out, lengths):
    rows, wide = tokens.shape
    depth, _, heads, hsize = w_qkv.shape
    half = depth // 2
    mine = lax.axis_index("gx")
    line = lax.axis_index("gy")
    chip, core = mine // 2, mine % 2
    where = jnp.stack([chip, core, line]).astype(jnp.int32)
    starts = (jnp.cumsum(lengths) - lengths).astype(jnp.int32)
    glob = mine * rows + jnp.arange(rows, dtype=jnp.int32)
    cosine, sine = tables(glob - begins(lengths, glob), hsize)
    cosine = jnp.concatenate([cosine, cosine], axis=1)
    sine = jnp.concatenate([-sine, sine], axis=1)

    flat = w_qkv.reshape(depth, -1)
    near, q1, cosine, sine, where = together(outer(tokens), inner(tokens), cosine, sine, where)
    q2, p2 = inner(near), outward(q1)
    w_x, w_y = swap(flat, 2), swap(flat, 4)

    upper, lower = halves(w_x, w_y)
    p3, far_a, far_b = outward(q2), swap(upper, 2), swap(lower, 4)
    x = normalize(where, (tokens, near, q1, p2, q2, p3), gain.reshape(LINE, 1, wide))
    held = (flat, w_x, w_y, far_a, far_b)
    weights = held + tuple(swap(w, 1) for w in held)
    sent = [None] * CHIPS
    for pair in PAIRS:
        sent[pair[0]], sent[pair[1]] = project(where, pair, x, cosine, sine, weights)
    keys, vals = [heads_in_order([a[j] for a in sent], chip) for j in (1, 2)]

    pieces = [sent[0]] + [swap(sent[m], 2 * m) for m in range(1, CHIPS)]
    *pieces, w_late = together(*pieces, w_out)
    w_x, w_y = swap(w_late, 2), swap(w_late, 4)
    heads_out = attend(
        where, starts, pieces + [swap(a, 1) for a in pieces], 1.0 / math.sqrt(hsize)
    )
    *heads_out, w_x, w_y = together(*heads_out, w_x, w_y)
    back = [heads_out[0]] + [swap(heads_out[m], 2 * m) for m in range(1, CHIPS)]
    attended = heads_in_order(back, chip)
    attended, w_x, w_y = together(attended, w_x, w_y)
    upper, lower = halves(w_x, w_y)
    near, q1, far_a, far_b = outer(attended), inner(attended), swap(upper, 2), swap(lower, 4)
    pieces = (w_late, w_x, w_y, far_a, far_b)
    q2, p2 = inner(near), outward(q1)
    others = [swap(w, 1) for w in pieces]
    p3 = outward(q2)
    total, w_last = early(where, (attended, near, q1, p2), (*pieces, *others))
    mixed = last(where, q2, p3, total, w_last)
    return (mixed, keys.reshape(rows, heads, hsize), vals.reshape(rows, heads, hsize))


def local(sizes, tokens, gain, w_qkv, w_out, lengths):
    heads = w_qkv.shape[2]
    fits = sizes == (2 * CHIPS, LINE) and heads == CHIPS and tokens.shape[1] == 2 * w_qkv.shape[0]
    plan = blocks_plan if fits else general
    return plan(tokens, gain, w_qkv, w_out, lengths)


def solution(mesh):
    sizes = (mesh.shape["gx"], mesh.shape["gy"])
    return jax.shard_map(
        functools.partial(local, sizes),
        mesh=mesh,
        in_specs=(P("gx", "gy"), P(), P("gx", None, "gy", None), P("gx", "gy"), P()),
        out_specs=(P("gx", "gy"), P("gx", "gy", None), P("gx", "gy", None)),
        check_vma=False,
    )
```

```python
import functools
import math

import jax
import jax.numpy as jnp
from jax import lax
from jax.experimental import pallas as pl
from jax.experimental.pallas import tpu as pltpu
from jax.sharding import PartitionSpec as P


def tables(position, hsize):
    half = hsize // 2
    freq = 10000.0 ** (-(2.0 * jnp.arange(half, dtype=jnp.float32)) / hsize)
    angle = position.astype(jnp.float32)[:, None] * freq[None, :]
    return jnp.cos(angle), jnp.sin(angle)


def rotate(vectors, position):
    half = vectors.shape[-1] // 2
    cosine, sine = tables(position, vectors.shape[-1])
    cosine, sine = cosine[:, None, :], sine[:, None, :]
    first = vectors[..., :half]
    second = vectors[..., half:]
    return jnp.concatenate(
        [first * cosine - second * sine, second * cosine + first * sine], axis=-1
    )


def begins(lengths, glob):
    doc_start = jnp.cumsum(lengths) - lengths
    return jnp.max(jnp.where(doc_start[None, :] <= glob[:, None], doc_start[None, :], 0), axis=1)


def block_rows(count):
    size = count
    while size > 1024 and size % 2 == 0:
        size = size // 2
    return size


def general(tokens, gain, w_qkv, w_out, lengths):
    tok_dev = tokens.shape[0]
    hloc = w_qkv.shape[2]
    hsize = w_qkv.shape[3]
    whole = lax.all_gather(tokens, "gy", axis=1, tiled=True)
    wide = whole.astype(jnp.float32)
    meansq = jnp.mean(wide * wide, axis=-1, keepdims=True)
    normed = (wide * lax.rsqrt(meansq + 1e-06) * gain[None, :]).astype(jnp.bfloat16)
    piece = lax.all_gather(w_qkv, "gx", axis=0, tiled=True)
    projected = jnp.dot(
        normed, piece.reshape(piece.shape[0], -1), preferred_element_type=jnp.float32
    )
    projected = projected.reshape(tok_dev, 3, hloc, hsize)
    mine = lax.axis_index("gx")
    glob = mine * tok_dev + jnp.arange(tok_dev, dtype=jnp.int32)
    begin = begins(lengths, glob)
    position = glob - begin
    query = rotate(projected[:, 0], position).astype(jnp.bfloat16)
    keys_own = rotate(projected[:, 1], position).astype(jnp.bfloat16)
    vals_own = projected[:, 2].astype(jnp.bfloat16)
    scale = 1.0 / math.sqrt(hsize)
    initial = (
        jnp.full((hloc, tok_dev), -1e30, jnp.float32),
        jnp.zeros((hloc, tok_dev), jnp.float32),
        jnp.zeros((hloc, tok_dev, hsize), jnp.float32),
    )
    keys_piece = lax.all_gather(keys_own, "gx", axis=0, tiled=True)
    vals_piece = lax.all_gather(vals_own, "gx", axis=0, tiled=True)
    count = keys_piece.shape[0]
    size = block_rows(count)

    def one_tile(number, state):
        running, totals, accum = state
        first = (number * size).astype(jnp.int32)
        keys_blk = lax.dynamic_slice_in_dim(keys_piece, first, size, 0)
        vals_blk = lax.dynamic_slice_in_dim(vals_piece, first, size, 0)
        kidx = first + jnp.arange(size, dtype=jnp.int32)
        score = (
            jnp.einsum("qhd,khd->hqk", query, keys_blk, preferred_element_type=jnp.float32) * scale
        )
        keep = (kidx[None, :] >= begin[:, None]) & (kidx[None, :] <= glob[:, None])
        score = jnp.where(keep[None], score, -1e30)
        newmax = jnp.maximum(running, jnp.max(score, axis=-1))
        weight = jnp.where(keep[None], jnp.exp(score - newmax[..., None]), 0.0)
        factor = jnp.exp(running - newmax)
        totals = totals * factor + jnp.sum(weight, axis=-1)
        update = jnp.einsum(
            "hqk,khd->hqd",
            weight.astype(jnp.bfloat16),
            vals_blk,
            preferred_element_type=jnp.float32,
        )
        accum = accum * factor[..., None] + update
        return (newmax, totals, accum)

    running, totals, accum = lax.fori_loop(0, count // size, one_tile, initial)
    attended = (accum / totals[..., None]).astype(jnp.bfloat16)
    attended = jnp.transpose(attended, (1, 0, 2)).reshape(tok_dev, hloc * hsize)
    all_heads = lax.all_gather(attended, "gy", axis=1, tiled=True)
    mixed = jnp.dot(
        all_heads, lax.all_gather(w_out, "gx", axis=0, tiled=True),
        preferred_element_type=jnp.float32,
    ).astype(jnp.bfloat16)
    return (mixed, keys_own, vals_own)


LINE = 4
CHIPS = 4
NORM_EFFORT = 8 << 30
PAIRS = ((1, 2), (3, 0))
KEYS = 512
EARLY_EFFORT = 1 << 30


def swap(x, mask):
    return lax.ppermute(x, "gx", [(i, i ^ mask) for i in range(2 * CHIPS)])


def outer(x):
    return lax.ppermute(x, "gy", [(0, 1), (1, 0), (2, 3), (3, 2)])


def inner(x):
    return lax.ppermute(x, "gy", [(1, 2), (2, 1)])


def outward(x):
    return lax.ppermute(x, "gy", [(1, 0), (2, 3)])


def order(line):
    low = line < 2
    return line ^ 1, jnp.where(low, 2, 1), jnp.where(low, 3, 0), (line == 0) | (line == LINE - 1)


def vmem():
    return pl.BlockSpec(memory_space=pltpu.VMEM)


def smem():
    return pl.BlockSpec(memory_space=pltpu.SMEM)


def hbm():
    return pl.BlockSpec(memory_space=pltpu.HBM)


def full(array):
    return pl.BlockSpec(array.shape, lambda *_: (0,) * array.ndim)


def effort(flops):
    return pl.CostEstimate(flops=flops, transcendentals=0, bytes_accessed=8 << 20)


def halves_kernel(x_ref, y_ref, upper_ref, lower_ref):
    upper_ref[...] = y_ref[...]
    lower_ref[...] = x_ref[...]


def halves(across, along):
    rows, cols = across.shape[0] // 2, across.shape[1]
    block = lambda half: pl.BlockSpec((rows, cols), lambda _: (half, 0))
    return pl.pallas_call(
        halves_kernel,
        grid=(1,),
        in_specs=[block(1), block(0)],
        out_specs=[block(0)] * 2,
        out_shape=[jax.ShapeDtypeStruct((rows, cols), across.dtype)] * 2,
        compiler_params=pltpu.CompilerParams(vmem_limit_bytes=6 << 20),
        name="halves",
    )(across, along)


def normalize_kernel(where_ref, *refs):
    blocks, (gain_ref, x_ref, raw_ref, sems) = refs[:6], refs[6:]
    chip, line = where_ref[0], where_ref[2]
    wide = raw_ref.shape[2]
    copies = [
        pltpu.make_async_copy(block, raw_ref.at[n], sems.at[n]) for n, block in enumerate(blocks)
    ]
    for copy in copies:
        copy.start()
    for copy in copies:
        copy.wait()
    own, near, q1, p2, q2, p3 = [raw_ref[n] for n in range(6)]
    second, third, fourth, end = order(line)
    raw = [
        own.astype(jnp.float32),
        near.astype(jnp.float32),
        jnp.where(end, p2, q1).astype(jnp.float32),
        jnp.where(end, p3, q2).astype(jnp.float32),
    ]
    square = sum(jnp.sum(r * r, axis=1, keepdims=True) for r in raw)
    scale = lax.rsqrt(square * (1.0 / (LINE * wide)) + 1e-06)
    for r, feature in zip(raw, (line, second, third, fourth)):
        normed = (r * scale * gain_ref[feature]).astype(jnp.bfloat16)
        x_ref[:, pl.ds(pl.multiple_of((feature ^ chip) * wide, wide), wide)] = normed


def normalize(where, blocks, gain):
    rows, wide = blocks[0].shape
    return pl.pallas_call(
        normalize_kernel,
        in_specs=[smem()] + [hbm()] * 6 + [vmem()],
        out_specs=vmem(),
        out_shape=jax.ShapeDtypeStruct((rows, LINE * wide), jnp.bfloat16),
        scratch_shapes=[pltpu.VMEM((6, rows, wide), jnp.bfloat16), pltpu.SemaphoreType.DMA((6,))],
        compiler_params=pltpu.CompilerParams(vmem_limit_bytes=12 << 20),
        cost_estimate=effort(NORM_EFFORT),
        name="normalize",
    )(where, *blocks, gain)


def head_columns(chip, pair, hsize):
    for i, m in enumerate(pair):
        for j in range(3):
            source = pl.multiple_of((CHIPS * j + (chip ^ m)) * hsize, hsize)
            yield pl.ds(source, hsize), slice((3 * i + j) * hsize, (3 * i + j + 1) * hsize)


def project_kernel(where_ref, x_ref, cos_ref, sin_ref, *refs, pair):
    weights, (out_a, out_b, w_ref) = refs[:10], refs[10:]
    chip, core = where_ref[0], where_ref[1]
    hsize = cos_ref.shape[1]
    depth = weights[0].shape[0]
    for source, target in head_columns(chip, pair, hsize):
        for side, half in ((0, core), (1, 1 - core)):
            for m in range(5):
                piece = weights[5 * side + m]
                row = (2 * min(m, 3) + half) * depth + (depth // 2 if m == 4 else 0)
                row = pl.multiple_of(row, depth // 2)
                w_ref[pl.ds(row, piece.shape[0]), target] = piece[:, source]
    total = jnp.dot(x_ref[...], w_ref[...], preferred_element_type=jnp.float32)
    for i, out in enumerate((out_a, out_b)):
        for j in range(3):
            u = total[:, (3 * i + j) * hsize : (3 * i + j + 1) * hsize]
            if j < 2:
                u = u * cos_ref[...] + pltpu.roll(u, hsize // 2, 1) * sin_ref[...]
            out[j] = u.astype(jnp.bfloat16)


def project(where, pair, x, cosine, sine, weights):
    rows, hsize = cosine.shape
    return pl.pallas_call(
        functools.partial(project_kernel, pair=pair),
        in_specs=[smem()] + [vmem()] * (3 + len(weights)),
        out_specs=[vmem()] * 2,
        out_shape=[jax.ShapeDtypeStruct((3, rows, hsize), jnp.bfloat16)] * 2,
        scratch_shapes=[pltpu.VMEM((x.shape[1], 6 * hsize), jnp.bfloat16)],
        compiler_params=pltpu.CompilerParams(vmem_limit_bytes=20 << 20),
        cost_estimate=effort(2 * x.size * 6 * hsize),
        name="project",
    )(where, x, cosine, sine, *weights)


def attend_kernel(where_ref, start_ref, *refs, scale):
    pieces, outs, (keys, vals) = refs[:8], refs[8:12], refs[12:]
    chip, core = where_ref[0], where_ref[1]
    _, rows, hsize = pieces[0].shape
    for cache in (keys, vals):
        cache[:KEYS] = jnp.zeros((KEYS, hsize), jnp.bfloat16)
    for side in range(2):
        for n in range(CHIPS):
            block = 2 * (chip ^ n) + (core if side == 0 else 1 - core)
            place = pl.ds(pl.multiple_of(KEYS + block * rows, 128), rows)
            keys[place, :] = pieces[CHIPS * side + n][1]
            vals[place, :] = pieces[CHIPS * side + n][2]
    for m in range(CHIPS):
        block = 2 * (chip ^ m) + core
        after = (block + 1) * rows
        query = pieces[m][0]
        qpos = block * rows + lax.broadcasted_iota(jnp.int32, (rows, 1), 0)
        begin = jnp.zeros((rows, 1), jnp.int32)
        lowest = jnp.int32(0)
        for d in range(start_ref.shape[0]):
            begin = jnp.where(start_ref[d] <= qpos, start_ref[d], begin)
            lowest = jnp.where(start_ref[d] <= block * rows, start_ref[d], lowest)

        def tile(number, state, after=after, query=query, qpos=qpos, begin=begin):
            running, totals, accum = state
            first = after - KEYS * (number + 1)
            place = pl.ds(pl.multiple_of(KEYS + first, 128), KEYS)
            kpos = first + lax.broadcasted_iota(jnp.int32, (1, KEYS), 1)
            score = scale * lax.dot_general(
                query, keys[place, :], (((1,), (1,)), ((), ())), preferred_element_type=jnp.float32
            )
            keep = (kpos >= begin) & (kpos <= qpos)
            score = jnp.where(keep, score, -1e30)
            newmax = jnp.maximum(running, jnp.max(score, axis=1, keepdims=True))
            weight = jnp.exp2(score - newmax)
            factor = jnp.exp2(running - newmax)
            totals = totals * factor + jnp.sum(weight, axis=1, keepdims=True)
            accum = accum * factor + jnp.dot(
                weight.astype(jnp.bfloat16), vals[place, :], preferred_element_type=jnp.float32
            )
            return newmax, totals, accum

        state = (
            jnp.full((rows, 1), -1e30, jnp.float32),
            jnp.zeros((rows, 1), jnp.float32),
            jnp.zeros((rows, hsize), jnp.float32),
        )
        tiles = lax.div(after - lowest + KEYS - 1, KEYS)
        running, totals, accum = lax.fori_loop(0, tiles, tile, state)
        outs[m][...] = (accum / totals).astype(jnp.bfloat16)


def attend(where, starts, pieces):
    _, rows, hsize = pieces[0].shape
    scale = math.log2(math.e) / math.sqrt(hsize)
    return pl.pallas_call(
        functools.partial(attend_kernel, scale=scale),
        in_specs=[smem()] * 2 + [vmem()] * len(pieces),
        out_specs=[vmem()] * CHIPS,
        out_shape=[jax.ShapeDtypeStruct((rows, hsize), jnp.bfloat16)] * CHIPS,
        scratch_shapes=[pltpu.VMEM((KEYS + 2 * CHIPS * rows, hsize), jnp.bfloat16)] * 2,
        compiler_params=pltpu.CompilerParams(vmem_limit_bytes=16 << 20),
        cost_estimate=effort(16 * 2 * rows * LINE * rows * hsize),
        name="attend",
    )(where, starts, *pieces)


def early_kernel(where_ref, own, near, q1, p2, *refs):
    pieces, total_ref, last_ref, w_ref = refs[:10], refs[10], refs[11], refs[12]
    chip, core, line = where_ref[0], where_ref[1], where_ref[2]
    depth = pieces[0].shape[0]
    for side in range(2):
        for m in range(CHIPS):
            block = 2 * (chip ^ m) + (core if side == 0 else 1 - core)
            if m < 3:
                w_ref[block] = pieces[5 * side + m][...]
            else:
                w_ref[block, : depth // 2] = pieces[5 * side + 3][...]
                w_ref[block, depth // 2 :] = pieces[5 * side + 4][...]

    def term(block, feature):
        return jnp.dot(
            block[:, :depth], w_ref[2 * feature], preferred_element_type=jnp.float32
        ) + jnp.dot(block[:, depth:], w_ref[2 * feature + 1], preferred_element_type=jnp.float32)

    second, third, fourth, end = order(line)
    total = term(own[...], line) + term(near[...], second)
    total_ref[...] = total + term(jnp.where(end, p2[...], q1[...]), third)
    last_ref[:depth] = w_ref[2 * fourth]
    last_ref[depth:] = w_ref[2 * fourth + 1]


def early(where, blocks, pieces):
    rows, wide = blocks[0].shape
    depth, cols = pieces[0].shape
    return pl.pallas_call(
        early_kernel,
        in_specs=[smem()] + [vmem()] * (len(blocks) + len(pieces)),
        out_specs=[vmem()] * 2,
        out_shape=[
            jax.ShapeDtypeStruct((rows, cols), jnp.float32),
            jax.ShapeDtypeStruct((wide, cols), jnp.bfloat16),
        ],
        scratch_shapes=[pltpu.VMEM((2 * CHIPS, depth, cols), jnp.bfloat16)],
        compiler_params=pltpu.CompilerParams(vmem_limit_bytes=16 << 20),
        cost_estimate=effort(EARLY_EFFORT),
        name="early",
    )(where, *blocks, *pieces)


def last_kernel(where_ref, q2, p3, total_ref, w_ref, out_ref):
    end = order(where_ref[2])[3]
    block = jnp.where(end, p3[...], q2[...])
    total = total_ref[...] + jnp.dot(block, w_ref[...], preferred_element_type=jnp.float32)
    out_ref[...] = total.astype(jnp.bfloat16)


def last(where, q2, p3, total, w_last):
    return pl.pallas_call(
        last_kernel,
        in_specs=[smem()] + [vmem()] * 4,
        out_specs=vmem(),
        out_shape=jax.ShapeDtypeStruct(total.shape, jnp.bfloat16),
        compiler_params=pltpu.CompilerParams(vmem_limit_bytes=8 << 20),
        cost_estimate=effort(2 * total.shape[0] * w_last.size),
        name="last",
    )(where, q2, p3, total, w_last)


def heads_in_order(back, chip):
    odd, high = (chip & 1) == 1, (chip & 2) == 2
    low, top = [
        jnp.concatenate([jnp.where(odd, b, a), jnp.where(odd, a, b)], axis=1)
        for a, b in (back[:2], back[2:])
    ]
    return jnp.concatenate([jnp.where(high, top, low), jnp.where(high, low, top)], axis=1)


def together(*arrays):
    return lax.optimization_barrier(arrays)


def blocks_plan(tokens, gain, w_qkv, w_out, lengths):
    rows, wide = tokens.shape
    depth, _, heads, hsize = w_qkv.shape
    mine = lax.axis_index("gx")
    line = lax.axis_index("gy")
    chip, core = mine // 2, mine % 2
    where = jnp.stack([chip, core, line]).astype(jnp.int32)
    starts = (jnp.cumsum(lengths) - lengths).astype(jnp.int32)
    glob = mine * rows + jnp.arange(rows, dtype=jnp.int32)
    cosine, sine = tables(glob - begins(lengths, glob), hsize)
    cosine = jnp.concatenate([cosine, cosine], axis=1)
    sine = jnp.concatenate([-sine, sine], axis=1)

    flat = w_qkv.reshape(depth, -1)
    near, q1, cosine, sine, where = together(outer(tokens), inner(tokens), cosine, sine, where)
    q2, p2 = inner(near), outward(q1)
    w_x, w_y = swap(flat, 2), swap(flat, 4)

    upper, lower = halves(w_x, w_y)
    p3, far_a, far_b = outward(q2), swap(upper, 2), swap(lower, 4)
    x = normalize(where, (tokens, near, q1, p2, q2, p3), gain.reshape(LINE, 1, wide))
    held = (flat, w_x, w_y, far_a, far_b)
    weights = held + tuple(swap(w, 1) for w in held)
    sent = [None] * CHIPS
    for pair in PAIRS:
        sent[pair[0]], sent[pair[1]] = project(where, pair, x, cosine, sine, weights)
    keys, vals = [heads_in_order([a[j] for a in sent], chip) for j in (1, 2)]

    pieces = [sent[0]] + [swap(sent[m], 2 * m) for m in range(1, CHIPS)]
    *pieces, w_late = together(*pieces, w_out)
    w_x, w_y = swap(w_late, 2), swap(w_late, 4)
    heads_out = attend(where, starts, pieces + [swap(a, 1) for a in pieces])
    *heads_out, w_x, w_y, w_other = together(*heads_out, w_x, w_y, swap(w_late, 1))
    back = [heads_out[0]] + [swap(heads_out[m], 2 * m) for m in range(1, CHIPS)]
    attended = heads_in_order(back, chip)
    attended, w_x, w_y = together(attended, w_x, w_y)
    upper, lower = halves(w_x, w_y)
    near, q1 = outer(attended), inner(attended)
    q1, upper, lower = together(q1, upper, lower)
    far_a, far_b = swap(upper, 2), swap(lower, 4)
    pieces = (w_late, w_x, w_y, far_a, far_b)
    q2, p2 = inner(near), outward(q1)
    others = [w_other] + [swap(w, 1) for w in pieces[1:]]
    p3 = outward(q2)
    total, w_last = early(where, (attended, near, q1, p2), (*pieces, *others))
    mixed = last(where, q2, p3, total, w_last)
    return (mixed, keys.reshape(rows, heads, hsize), vals.reshape(rows, heads, hsize))


def local(sizes, tokens, gain, w_qkv, w_out, lengths):
    heads = w_qkv.shape[2]
    fits = sizes == (2 * CHIPS, LINE) and heads == CHIPS and tokens.shape[1] == 2 * w_qkv.shape[0]
    plan = blocks_plan if fits else general
    return plan(tokens, gain, w_qkv, w_out, lengths)


def solution(mesh):
    sizes = (mesh.shape["gx"], mesh.shape["gy"])
    return jax.shard_map(
        functools.partial(local, sizes),
        mesh=mesh,
        in_specs=(P("gx", "gy"), P(), P("gx", None, "gy", None), P("gx", "gy"), P()),
        out_specs=(P("gx", "gy"), P("gx", "gy", None), P("gx", "gy", None)),
        check_vma=False,
    )
```

```python
import functools
import math

import jax
import jax.numpy as jnp
from jax import lax
from jax.experimental import pallas as pl
from jax.experimental.pallas import tpu as pltpu
from jax.sharding import PartitionSpec as P


def tables(position, hsize):
    half = hsize // 2
    freq = 10000.0 ** (-(2.0 * jnp.arange(half, dtype=jnp.float32)) / hsize)
    angle = position.astype(jnp.float32)[:, None] * freq[None, :]
    return jnp.cos(angle), jnp.sin(angle)


def rotate(vectors, position):
    half = vectors.shape[-1] // 2
    cosine, sine = tables(position, vectors.shape[-1])
    cosine, sine = cosine[:, None, :], sine[:, None, :]
    first = vectors[..., :half]
    second = vectors[..., half:]
    return jnp.concatenate(
        [first * cosine - second * sine, second * cosine + first * sine], axis=-1
    )


def begins(lengths, glob):
    doc_start = jnp.cumsum(lengths) - lengths
    return jnp.max(jnp.where(doc_start[None, :] <= glob[:, None], doc_start[None, :], 0), axis=1)


def block_rows(count):
    size = count
    while size > 1024 and size % 2 == 0:
        size = size // 2
    return size


def general(tokens, gain, w_qkv, w_out, lengths):
    tok_dev = tokens.shape[0]
    hloc = w_qkv.shape[2]
    hsize = w_qkv.shape[3]
    whole = lax.all_gather(tokens, "gy", axis=1, tiled=True)
    wide = whole.astype(jnp.float32)
    meansq = jnp.mean(wide * wide, axis=-1, keepdims=True)
    normed = (wide * lax.rsqrt(meansq + 1e-06) * gain[None, :]).astype(jnp.bfloat16)
    piece = lax.all_gather(w_qkv, "gx", axis=0, tiled=True)
    projected = jnp.dot(
        normed, piece.reshape(piece.shape[0], -1), preferred_element_type=jnp.float32
    )
    projected = projected.reshape(tok_dev, 3, hloc, hsize)
    mine = lax.axis_index("gx")
    glob = mine * tok_dev + jnp.arange(tok_dev, dtype=jnp.int32)
    begin = begins(lengths, glob)
    position = glob - begin
    query = rotate(projected[:, 0], position).astype(jnp.bfloat16)
    keys_own = rotate(projected[:, 1], position).astype(jnp.bfloat16)
    vals_own = projected[:, 2].astype(jnp.bfloat16)
    scale = 1.0 / math.sqrt(hsize)
    initial = (
        jnp.full((hloc, tok_dev), -1e30, jnp.float32),
        jnp.zeros((hloc, tok_dev), jnp.float32),
        jnp.zeros((hloc, tok_dev, hsize), jnp.float32),
    )
    keys_piece = lax.all_gather(keys_own, "gx", axis=0, tiled=True)
    vals_piece = lax.all_gather(vals_own, "gx", axis=0, tiled=True)
    count = keys_piece.shape[0]
    size = block_rows(count)

    def one_tile(number, state):
        running, totals, accum = state
        first = (number * size).astype(jnp.int32)
        keys_blk = lax.dynamic_slice_in_dim(keys_piece, first, size, 0)
        vals_blk = lax.dynamic_slice_in_dim(vals_piece, first, size, 0)
        kidx = first + jnp.arange(size, dtype=jnp.int32)
        score = (
            jnp.einsum("qhd,khd->hqk", query, keys_blk, preferred_element_type=jnp.float32) * scale
        )
        keep = (kidx[None, :] >= begin[:, None]) & (kidx[None, :] <= glob[:, None])
        score = jnp.where(keep[None], score, -1e30)
        newmax = jnp.maximum(running, jnp.max(score, axis=-1))
        weight = jnp.where(keep[None], jnp.exp(score - newmax[..., None]), 0.0)
        factor = jnp.exp(running - newmax)
        totals = totals * factor + jnp.sum(weight, axis=-1)
        update = jnp.einsum(
            "hqk,khd->hqd",
            weight.astype(jnp.bfloat16),
            vals_blk,
            preferred_element_type=jnp.float32,
        )
        accum = accum * factor[..., None] + update
        return (newmax, totals, accum)

    running, totals, accum = lax.fori_loop(0, count // size, one_tile, initial)
    attended = (accum / totals[..., None]).astype(jnp.bfloat16)
    attended = jnp.transpose(attended, (1, 0, 2)).reshape(tok_dev, hloc * hsize)
    all_heads = lax.all_gather(attended, "gy", axis=1, tiled=True)
    mixed = jnp.dot(
        all_heads, lax.all_gather(w_out, "gx", axis=0, tiled=True),
        preferred_element_type=jnp.float32,
    ).astype(jnp.bfloat16)
    return (mixed, keys_own, vals_own)


LINE = 4
CHIPS = 4
NORM_EFFORT = 8 << 30
PAIRS = ((1, 2), (3, 0))
KEYS = 512
EARLY_EFFORT = 1 << 30


def swap(x, mask):
    return lax.ppermute(x, "gx", [(i, i ^ mask) for i in range(2 * CHIPS)])


def outer(x):
    return lax.ppermute(x, "gy", [(0, 1), (1, 0), (2, 3), (3, 2)])


def inner(x):
    return lax.ppermute(x, "gy", [(1, 2), (2, 1)])


def outward(x):
    return lax.ppermute(x, "gy", [(1, 0), (2, 3)])


def order(line):
    low = line < 2
    return line ^ 1, jnp.where(low, 2, 1), jnp.where(low, 3, 0), (line == 0) | (line == LINE - 1)


def vmem():
    return pl.BlockSpec(memory_space=pltpu.VMEM)


def smem():
    return pl.BlockSpec(memory_space=pltpu.SMEM)


def hbm():
    return pl.BlockSpec(memory_space=pltpu.HBM)


def full(array):
    return pl.BlockSpec(array.shape, lambda *_: (0,) * array.ndim)


def effort(flops):
    return pl.CostEstimate(flops=flops, transcendentals=0, bytes_accessed=8 << 20)


def halves_kernel(x_ref, y_ref, upper_ref, lower_ref):
    upper_ref[...] = y_ref[...]
    lower_ref[...] = x_ref[...]


def halves(across, along):
    rows, cols = across.shape[0] // 2, across.shape[1]
    block = lambda half: pl.BlockSpec((rows, cols), lambda _: (half, 0))
    return pl.pallas_call(
        halves_kernel,
        grid=(1,),
        in_specs=[block(1), block(0)],
        out_specs=[block(0)] * 2,
        out_shape=[jax.ShapeDtypeStruct((rows, cols), across.dtype)] * 2,
        compiler_params=pltpu.CompilerParams(vmem_limit_bytes=6 << 20),
        name="halves",
    )(across, along)


def normalize_kernel(where_ref, *refs):
    blocks, (gain_ref, x_ref, raw_ref, sems) = refs[:6], refs[6:]
    chip, line = where_ref[0], where_ref[2]
    wide = raw_ref.shape[2]
    copies = [
        pltpu.make_async_copy(block, raw_ref.at[n], sems.at[n]) for n, block in enumerate(blocks)
    ]
    for copy in copies:
        copy.start()
    for copy in copies:
        copy.wait()
    own, near, q1, p2, q2, p3 = [raw_ref[n] for n in range(6)]
    second, third, fourth, end = order(line)
    raw = [
        own.astype(jnp.float32),
        near.astype(jnp.float32),
        jnp.where(end, p2, q1).astype(jnp.float32),
        jnp.where(end, p3, q2).astype(jnp.float32),
    ]
    square = sum(jnp.sum(r * r, axis=1, keepdims=True) for r in raw)
    scale = lax.rsqrt(square * (1.0 / (LINE * wide)) + 1e-06)
    for r, feature in zip(raw, (line, second, third, fourth)):
        normed = (r * scale * gain_ref[feature]).astype(jnp.bfloat16)
        x_ref[:, pl.ds(pl.multiple_of((feature ^ chip) * wide, wide), wide)] = normed


def normalize(where, blocks, gain):
    rows, wide = blocks[0].shape
    return pl.pallas_call(
        normalize_kernel,
        in_specs=[smem()] + [hbm()] * 6 + [vmem()],
        out_specs=vmem(),
        out_shape=jax.ShapeDtypeStruct((rows, LINE * wide), jnp.bfloat16),
        scratch_shapes=[pltpu.VMEM((6, rows, wide), jnp.bfloat16), pltpu.SemaphoreType.DMA((6,))],
        compiler_params=pltpu.CompilerParams(vmem_limit_bytes=12 << 20),
        cost_estimate=effort(NORM_EFFORT),
        name="normalize",
    )(where, *blocks, gain)


def head_columns(chip, pair, hsize):
    for i, m in enumerate(pair):
        for j in range(3):
            source = pl.multiple_of((CHIPS * j + (chip ^ m)) * hsize, hsize)
            yield pl.ds(source, hsize), slice((3 * i + j) * hsize, (3 * i + j + 1) * hsize)


def project_kernel(where_ref, x_ref, cos_ref, sin_ref, *refs, pair):
    weights, (out_a, out_b, w_ref) = refs[:10], refs[10:]
    chip, core = where_ref[0], where_ref[1]
    hsize = cos_ref.shape[1]
    depth = weights[0].shape[0]
    for source, target in head_columns(chip, pair, hsize):
        for side, half in ((0, core), (1, 1 - core)):
            for m in range(5):
                piece = weights[5 * side + m]
                row = (2 * min(m, 3) + half) * depth + (depth // 2 if m == 4 else 0)
                row = pl.multiple_of(row, depth // 2)
                w_ref[pl.ds(row, piece.shape[0]), target] = piece[:, source]
    total = jnp.dot(x_ref[...], w_ref[...], preferred_element_type=jnp.float32)
    for i, out in enumerate((out_a, out_b)):
        for j in range(3):
            u = total[:, (3 * i + j) * hsize : (3 * i + j + 1) * hsize]
            if j < 2:
                u = u * cos_ref[...] + pltpu.roll(u, hsize // 2, 1) * sin_ref[...]
            out[j] = u.astype(jnp.bfloat16)


def project(where, pair, x, cosine, sine, weights):
    rows, hsize = cosine.shape
    return pl.pallas_call(
        functools.partial(project_kernel, pair=pair),
        in_specs=[smem()] + [vmem()] * (3 + len(weights)),
        out_specs=[vmem()] * 2,
        out_shape=[jax.ShapeDtypeStruct((3, rows, hsize), jnp.bfloat16)] * 2,
        scratch_shapes=[pltpu.VMEM((x.shape[1], 6 * hsize), jnp.bfloat16)],
        compiler_params=pltpu.CompilerParams(vmem_limit_bytes=20 << 20),
        cost_estimate=effort(2 * x.size * 6 * hsize),
        name="project",
    )(where, x, cosine, sine, *weights)


def attend_kernel(where_ref, start_ref, *refs, scale):
    pieces, outs, (keys, vals) = refs[:8], refs[8:12], refs[12:]
    chip, core = where_ref[0], where_ref[1]
    _, rows, hsize = pieces[0].shape
    for cache in (keys, vals):
        cache[:KEYS] = jnp.zeros((KEYS, hsize), jnp.bfloat16)
    for side in range(2):
        for n in range(CHIPS):
            block = 2 * (chip ^ n) + (core if side == 0 else 1 - core)
            place = pl.ds(pl.multiple_of(KEYS + block * rows, 128), rows)
            keys[place, :] = pieces[CHIPS * side + n][1]
            vals[place, :] = pieces[CHIPS * side + n][2]
    for m in range(CHIPS):
        block = 2 * (chip ^ m) + core
        after = (block + 1) * rows
        query = pieces[m][0]
        qpos = block * rows + lax.broadcasted_iota(jnp.int32, (rows, 1), 0)
        begin = jnp.zeros((rows, 1), jnp.int32)
        lowest = jnp.int32(0)
        for d in range(start_ref.shape[0]):
            begin = jnp.where(start_ref[d] <= qpos, start_ref[d], begin)
            lowest = jnp.where(start_ref[d] <= block * rows, start_ref[d], lowest)

        def tile(number, state, after=after, query=query, qpos=qpos, begin=begin):
            running, totals, accum = state
            first = after - KEYS * (number + 1)
            place = pl.ds(pl.multiple_of(KEYS + first, 128), KEYS)
            kpos = first + lax.broadcasted_iota(jnp.int32, (1, KEYS), 1)
            score = scale * lax.dot_general(
                query, keys[place, :], (((1,), (1,)), ((), ())), preferred_element_type=jnp.float32
            )
            keep = (kpos >= begin) & (kpos <= qpos)
            score = jnp.where(keep, score, -1e30)
            newmax = jnp.maximum(running, jnp.max(score, axis=1, keepdims=True))
            weight = jnp.exp2(score - newmax)
            factor = jnp.exp2(running - newmax)
            totals = totals * factor + jnp.sum(weight, axis=1, keepdims=True)
            accum = accum * factor + jnp.dot(
                weight.astype(jnp.bfloat16), vals[place, :], preferred_element_type=jnp.float32
            )
            return newmax, totals, accum

        state = (
            jnp.full((rows, 1), -1e30, jnp.float32),
            jnp.zeros((rows, 1), jnp.float32),
            jnp.zeros((rows, hsize), jnp.float32),
        )
        tiles = lax.div(after - lowest + KEYS - 1, KEYS)
        running, totals, accum = lax.fori_loop(0, tiles, tile, state)
        outs[m][...] = (accum / totals).astype(jnp.bfloat16)


def attend(where, starts, pieces):
    _, rows, hsize = pieces[0].shape
    scale = math.log2(math.e) / math.sqrt(hsize)
    return pl.pallas_call(
        functools.partial(attend_kernel, scale=scale),
        in_specs=[smem()] * 2 + [vmem()] * len(pieces),
        out_specs=[vmem()] * CHIPS,
        out_shape=[jax.ShapeDtypeStruct((rows, hsize), jnp.bfloat16)] * CHIPS,
        scratch_shapes=[pltpu.VMEM((KEYS + 2 * CHIPS * rows, hsize), jnp.bfloat16)] * 2,
        compiler_params=pltpu.CompilerParams(vmem_limit_bytes=16 << 20),
        cost_estimate=effort(16 * 2 * rows * LINE * rows * hsize),
        name="attend",
    )(where, starts, *pieces)


def early_kernel(where_ref, own, near, q1, p2, *refs):
    pieces, total_ref, last_ref, w_ref = refs[:10], refs[10], refs[11], refs[12]
    chip, core, line = where_ref[0], where_ref[1], where_ref[2]
    depth = pieces[0].shape[0]
    for side in range(2):
        for m in range(CHIPS):
            block = 2 * (chip ^ m) + (core if side == 0 else 1 - core)
            if m < 3:
                w_ref[block] = pieces[5 * side + m][...]
            else:
                w_ref[block, : depth // 2] = pieces[5 * side + 3][...]
                w_ref[block, depth // 2 :] = pieces[5 * side + 4][...]

    def term(block, feature):
        return jnp.dot(
            block[:, :depth], w_ref[2 * feature], preferred_element_type=jnp.float32
        ) + jnp.dot(block[:, depth:], w_ref[2 * feature + 1], preferred_element_type=jnp.float32)

    second, third, fourth, end = order(line)
    total = term(own[...], line) + term(near[...], second)
    total_ref[...] = total + term(jnp.where(end, p2[...], q1[...]), third)
    last_ref[:depth] = w_ref[2 * fourth]
    last_ref[depth:] = w_ref[2 * fourth + 1]


def early(where, blocks, pieces):
    rows, wide = blocks[0].shape
    depth, cols = pieces[0].shape
    return pl.pallas_call(
        early_kernel,
        in_specs=[smem()] + [vmem()] * (len(blocks) + len(pieces)),
        out_specs=[vmem()] * 2,
        out_shape=[
            jax.ShapeDtypeStruct((rows, cols), jnp.float32),
            jax.ShapeDtypeStruct((wide, cols), jnp.bfloat16),
        ],
        scratch_shapes=[pltpu.VMEM((2 * CHIPS, depth, cols), jnp.bfloat16)],
        compiler_params=pltpu.CompilerParams(vmem_limit_bytes=16 << 20),
        cost_estimate=effort(EARLY_EFFORT),
        name="early",
    )(where, *blocks, *pieces)


def last_kernel(where_ref, q2, p3, total_ref, w_ref, out_ref):
    end = order(where_ref[2])[3]
    block = jnp.where(end, p3[...], q2[...])
    total = total_ref[...] + jnp.dot(block, w_ref[...], preferred_element_type=jnp.float32)
    out_ref[...] = total.astype(jnp.bfloat16)


def last(where, q2, p3, total, w_last):
    return pl.pallas_call(
        last_kernel,
        in_specs=[smem()] + [vmem()] * 4,
        out_specs=vmem(),
        out_shape=jax.ShapeDtypeStruct(total.shape, jnp.bfloat16),
        compiler_params=pltpu.CompilerParams(vmem_limit_bytes=8 << 20),
        cost_estimate=effort(2 * total.shape[0] * w_last.size),
        name="last",
    )(where, q2, p3, total, w_last)


def heads_in_order(back, chip):
    odd, high = (chip & 1) == 1, (chip & 2) == 2
    low, top = [
        jnp.concatenate([jnp.where(odd, b, a), jnp.where(odd, a, b)], axis=1)
        for a, b in (back[:2], back[2:])
    ]
    return jnp.concatenate([jnp.where(high, top, low), jnp.where(high, low, top)], axis=1)


def together(*arrays):
    return lax.optimization_barrier(arrays)


def blocks_plan(tokens, gain, w_qkv, w_out, lengths):
    rows, wide = tokens.shape
    depth, _, heads, hsize = w_qkv.shape
    mine = lax.axis_index("gx")
    line = lax.axis_index("gy")
    chip, core = mine // 2, mine % 2
    where = jnp.stack([chip, core, line]).astype(jnp.int32)
    starts = (jnp.cumsum(lengths) - lengths).astype(jnp.int32)
    glob = mine * rows + jnp.arange(rows, dtype=jnp.int32)
    cosine, sine = tables(glob - begins(lengths, glob), hsize)
    cosine = jnp.concatenate([cosine, cosine], axis=1)
    sine = jnp.concatenate([-sine, sine], axis=1)

    flat = w_qkv.reshape(depth, -1)
    near, q1, cosine, sine, where = together(outer(tokens), inner(tokens), cosine, sine, where)
    q2, p2 = inner(near), outward(q1)
    w_x, w_y = swap(flat, 2), swap(flat, 4)

    upper, lower = halves(w_x, w_y)
    p3, far_a, far_b = outward(q2), swap(upper, 2), swap(lower, 4)
    x = normalize(where, (tokens, near, q1, p2, q2, p3), gain.reshape(LINE, 1, wide))
    held = (flat, w_x, w_y, far_a, far_b)
    weights = held + tuple(swap(w, 1) for w in held)
    sent = [None] * CHIPS
    for pair in PAIRS:
        sent[pair[0]], sent[pair[1]] = project(where, pair, x, cosine, sine, weights)
    keys, vals = [heads_in_order([a[j] for a in sent], chip) for j in (1, 2)]

    pieces = [sent[0]] + [swap(sent[m], 2 * m) for m in range(1, CHIPS)]
    heads_out = attend(where, starts, pieces + [swap(a, 1) for a in pieces])
    back = [heads_out[0]] + [swap(heads_out[m], 2 * m) for m in range(1, CHIPS)]

    attended, w_late = together(heads_in_order(back, chip), w_out)
    near, q1 = outer(attended), inner(attended)
    w_x, w_y = swap(w_late, 2), swap(w_late, 4)
    upper, lower = halves(w_x, w_y)
    q1, upper, lower = together(q1, upper, lower)
    far_a, far_b = swap(upper, 2), swap(lower, 4)
    pieces = (w_late, w_x, w_y, far_a, far_b)
    q2, p2 = inner(near), outward(q1)
    p3 = outward(q2)
    pieces = pieces + tuple(swap(w, 1) for w in pieces)
    total, w_last = early(where, (attended, near, q1, p2), pieces)
    mixed = last(where, q2, p3, total, w_last)
    return (mixed, keys.reshape(rows, heads, hsize), vals.reshape(rows, heads, hsize))


def local(sizes, tokens, gain, w_qkv, w_out, lengths):
    heads = w_qkv.shape[2]
    fits = sizes == (2 * CHIPS, LINE) and heads == CHIPS and tokens.shape[1] == 2 * w_qkv.shape[0]
    plan = blocks_plan if fits else general
    return plan(tokens, gain, w_qkv, w_out, lengths)


def solution(mesh):
    sizes = (mesh.shape["gx"], mesh.shape["gy"])
    return jax.shard_map(
        functools.partial(local, sizes),
        mesh=mesh,
        in_specs=(P("gx", "gy"), P(), P("gx", None, "gy", None), P("gx", "gy"), P()),
        out_specs=(P("gx", "gy"), P("gx", "gy", None), P("gx", "gy", None)),
        check_vma=False,
    )
```

```python
import functools
import math

import jax
import jax.numpy as jnp
from jax import lax
from jax.experimental import pallas as pl
from jax.experimental.pallas import tpu as pltpu
from jax.sharding import PartitionSpec as P


def tables(position, hsize):
    half = hsize // 2
    freq = 10000.0 ** (-(2.0 * jnp.arange(half, dtype=jnp.float32)) / hsize)
    angle = position.astype(jnp.float32)[:, None] * freq[None, :]
    return jnp.cos(angle), jnp.sin(angle)


def rotate(vectors, position):
    half = vectors.shape[-1] // 2
    cosine, sine = tables(position, vectors.shape[-1])
    cosine, sine = cosine[:, None, :], sine[:, None, :]
    first = vectors[..., :half]
    second = vectors[..., half:]
    return jnp.concatenate(
        [first * cosine - second * sine, second * cosine + first * sine], axis=-1
    )


def begins(lengths, glob):
    doc_start = jnp.cumsum(lengths) - lengths
    return jnp.max(jnp.where(doc_start[None, :] <= glob[:, None], doc_start[None, :], 0), axis=1)


def block_rows(count):
    size = count
    while size > 1024 and size % 2 == 0:
        size = size // 2
    return size


def general(tokens, gain, w_qkv, w_out, lengths):
    tok_dev = tokens.shape[0]
    hloc = w_qkv.shape[2]
    hsize = w_qkv.shape[3]
    whole = lax.all_gather(tokens, "gy", axis=1, tiled=True)
    wide = whole.astype(jnp.float32)
    meansq = jnp.mean(wide * wide, axis=-1, keepdims=True)
    normed = (wide * lax.rsqrt(meansq + 1e-06) * gain[None, :]).astype(jnp.bfloat16)
    piece = lax.all_gather(w_qkv, "gx", axis=0, tiled=True)
    projected = jnp.dot(
        normed, piece.reshape(piece.shape[0], -1), preferred_element_type=jnp.float32
    )
    projected = projected.reshape(tok_dev, 3, hloc, hsize)
    mine = lax.axis_index("gx")
    glob = mine * tok_dev + jnp.arange(tok_dev, dtype=jnp.int32)
    begin = begins(lengths, glob)
    position = glob - begin
    query = rotate(projected[:, 0], position).astype(jnp.bfloat16)
    keys_own = rotate(projected[:, 1], position).astype(jnp.bfloat16)
    vals_own = projected[:, 2].astype(jnp.bfloat16)
    scale = 1.0 / math.sqrt(hsize)
    initial = (
        jnp.full((hloc, tok_dev), -1e30, jnp.float32),
        jnp.zeros((hloc, tok_dev), jnp.float32),
        jnp.zeros((hloc, tok_dev, hsize), jnp.float32),
    )
    keys_piece = lax.all_gather(keys_own, "gx", axis=0, tiled=True)
    vals_piece = lax.all_gather(vals_own, "gx", axis=0, tiled=True)
    count = keys_piece.shape[0]
    size = block_rows(count)

    def one_tile(number, state):
        running, totals, accum = state
        first = (number * size).astype(jnp.int32)
        keys_blk = lax.dynamic_slice_in_dim(keys_piece, first, size, 0)
        vals_blk = lax.dynamic_slice_in_dim(vals_piece, first, size, 0)
        kidx = first + jnp.arange(size, dtype=jnp.int32)
        score = (
            jnp.einsum("qhd,khd->hqk", query, keys_blk, preferred_element_type=jnp.float32) * scale
        )
        keep = (kidx[None, :] >= begin[:, None]) & (kidx[None, :] <= glob[:, None])
        score = jnp.where(keep[None], score, -1e30)
        newmax = jnp.maximum(running, jnp.max(score, axis=-1))
        weight = jnp.where(keep[None], jnp.exp(score - newmax[..., None]), 0.0)
        factor = jnp.exp(running - newmax)
        totals = totals * factor + jnp.sum(weight, axis=-1)
        update = jnp.einsum(
            "hqk,khd->hqd",
            weight.astype(jnp.bfloat16),
            vals_blk,
            preferred_element_type=jnp.float32,
        )
        accum = accum * factor[..., None] + update
        return (newmax, totals, accum)

    running, totals, accum = lax.fori_loop(0, count // size, one_tile, initial)
    attended = (accum / totals[..., None]).astype(jnp.bfloat16)
    attended = jnp.transpose(attended, (1, 0, 2)).reshape(tok_dev, hloc * hsize)
    all_heads = lax.all_gather(attended, "gy", axis=1, tiled=True)
    mixed = jnp.dot(
        all_heads, lax.all_gather(w_out, "gx", axis=0, tiled=True),
        preferred_element_type=jnp.float32,
    ).astype(jnp.bfloat16)
    return (mixed, keys_own, vals_own)


LINE = 4
CHIPS = 4
NORM_EFFORT = 8 << 30
PAIRS = ((1, 2), (3, 0))
KEYS = 512
EARLY_EFFORT = 1 << 30


def swap(x, mask):
    return lax.ppermute(x, "gx", [(i, i ^ mask) for i in range(2 * CHIPS)])


def outer(x):
    return lax.ppermute(x, "gy", [(0, 1), (1, 0), (2, 3), (3, 2)])


def inner(x):
    return lax.ppermute(x, "gy", [(1, 2), (2, 1)])


def outward(x):
    return lax.ppermute(x, "gy", [(1, 0), (2, 3)])


def order(line):
    low = line < 2
    return line ^ 1, jnp.where(low, 2, 1), jnp.where(low, 3, 0), (line == 0) | (line == LINE - 1)


def vmem():
    return pl.BlockSpec(memory_space=pltpu.VMEM)


def smem():
    return pl.BlockSpec(memory_space=pltpu.SMEM)


def hbm():
    return pl.BlockSpec(memory_space=pltpu.HBM)


def full(array):
    return pl.BlockSpec(array.shape, lambda *_: (0,) * array.ndim)


def effort(flops):
    return pl.CostEstimate(flops=flops, transcendentals=0, bytes_accessed=8 << 20)


def halves_kernel(x_ref, y_ref, upper_ref, lower_ref):
    upper_ref[...] = y_ref[...]
    lower_ref[...] = x_ref[...]


def halves(across, along):
    rows, cols = across.shape[0] // 2, across.shape[1]
    block = lambda half: pl.BlockSpec((rows, cols), lambda _: (half, 0))
    return pl.pallas_call(
        halves_kernel,
        grid=(1,),
        in_specs=[block(1), block(0)],
        out_specs=[block(0)] * 2,
        out_shape=[jax.ShapeDtypeStruct((rows, cols), across.dtype)] * 2,
        compiler_params=pltpu.CompilerParams(vmem_limit_bytes=6 << 20),
        name="halves",
    )(across, along)


def normalize_kernel(where_ref, *refs):
    blocks, (gain_ref, x_ref) = refs[:6], refs[6:]
    chip, line = where_ref[0], where_ref[2]
    wide = blocks[0].shape[1]
    own, near, q1, p2, q2, p3 = [block[...] for block in blocks]
    second, third, fourth, end = order(line)
    raw = [
        own.astype(jnp.float32),
        near.astype(jnp.float32),
        jnp.where(end, p2, q1).astype(jnp.float32),
        jnp.where(end, p3, q2).astype(jnp.float32),
    ]
    square = sum(jnp.sum(r * r, axis=1, keepdims=True) for r in raw)
    scale = lax.rsqrt(square * (1.0 / (LINE * wide)) + 1e-06)
    for r, feature in zip(raw, (line, second, third, fourth)):
        normed = (r * scale * gain_ref[feature]).astype(jnp.bfloat16)
        x_ref[:, pl.ds(pl.multiple_of((feature ^ chip) * wide, wide), wide)] = normed


def normalize(where, blocks, gain):
    rows, wide = blocks[0].shape
    return pl.pallas_call(
        normalize_kernel,
        in_specs=[smem()] + [vmem()] * 7,
        out_specs=vmem(),
        out_shape=jax.ShapeDtypeStruct((rows, LINE * wide), jnp.bfloat16),
        compiler_params=pltpu.CompilerParams(vmem_limit_bytes=12 << 20),
        cost_estimate=effort(NORM_EFFORT),
        name="normalize",
    )(where, *blocks, gain)


def head_columns(chip, pair, hsize):
    for i, m in enumerate(pair):
        for j in range(3):
            source = pl.multiple_of((CHIPS * j + (chip ^ m)) * hsize, hsize)
            yield pl.ds(source, hsize), slice((3 * i + j) * hsize, (3 * i + j + 1) * hsize)


def project_kernel(where_ref, x_ref, cos_ref, sin_ref, *refs, pair):
    weights, (out_a, out_b, w_ref) = refs[:10], refs[10:]
    chip, core = where_ref[0], where_ref[1]
    hsize = cos_ref.shape[1]
    depth = weights[0].shape[0]
    for source, target in head_columns(chip, pair, hsize):
        for side, half in ((0, core), (1, 1 - core)):
            for m in range(5):
                piece = weights[5 * side + m]
                row = (2 * min(m, 3) + half) * depth + (depth // 2 if m == 4 else 0)
                row = pl.multiple_of(row, depth // 2)
                w_ref[pl.ds(row, piece.shape[0]), target] = piece[:, source]
    total = jnp.dot(x_ref[...], w_ref[...], preferred_element_type=jnp.float32)
    for i, out in enumerate((out_a, out_b)):
        for j in range(3):
            u = total[:, (3 * i + j) * hsize : (3 * i + j + 1) * hsize]
            if j < 2:
                u = u * cos_ref[...] + pltpu.roll(u, hsize // 2, 1) * sin_ref[...]
            out[j] = u.astype(jnp.bfloat16)


def project(where, pair, x, cosine, sine, weights):
    rows, hsize = cosine.shape
    return pl.pallas_call(
        functools.partial(project_kernel, pair=pair),
        in_specs=[smem()] + [vmem()] * (3 + len(weights)),
        out_specs=[vmem()] * 2,
        out_shape=[jax.ShapeDtypeStruct((3, rows, hsize), jnp.bfloat16)] * 2,
        scratch_shapes=[pltpu.VMEM((x.shape[1], 6 * hsize), jnp.bfloat16)],
        compiler_params=pltpu.CompilerParams(vmem_limit_bytes=20 << 20),
        cost_estimate=effort(2 * x.size * 6 * hsize),
        name="project",
    )(where, x, cosine, sine, *weights)


def attend_kernel(where_ref, start_ref, *refs, scale):
    pieces, outs, (keys, vals) = refs[:8], refs[8:12], refs[12:]
    chip, core = where_ref[0], where_ref[1]
    _, rows, hsize = pieces[0].shape
    for cache in (keys, vals):
        cache[:KEYS] = jnp.zeros((KEYS, hsize), jnp.bfloat16)
    for side in range(2):
        for n in range(CHIPS):
            block = 2 * (chip ^ n) + (core if side == 0 else 1 - core)
            place = pl.ds(pl.multiple_of(KEYS + block * rows, 128), rows)
            keys[place, :] = pieces[CHIPS * side + n][1]
            vals[place, :] = pieces[CHIPS * side + n][2]
    for m in range(CHIPS):
        block = 2 * (chip ^ m) + core
        after = (block + 1) * rows
        query = pieces[m][0]
        qpos = block * rows + lax.broadcasted_iota(jnp.int32, (rows, 1), 0)
        begin = jnp.zeros((rows, 1), jnp.int32)
        lowest = jnp.int32(0)
        for d in range(start_ref.shape[0]):
            begin = jnp.where(start_ref[d] <= qpos, start_ref[d], begin)
            lowest = jnp.where(start_ref[d] <= block * rows, start_ref[d], lowest)

        def tile(number, state, after=after, query=query, qpos=qpos, begin=begin):
            running, totals, accum = state
            first = after - KEYS * (number + 1)
            place = pl.ds(pl.multiple_of(KEYS + first, 128), KEYS)
            kpos = first + lax.broadcasted_iota(jnp.int32, (1, KEYS), 1)
            score = scale * lax.dot_general(
                query, keys[place, :], (((1,), (1,)), ((), ())), preferred_element_type=jnp.float32
            )
            keep = (kpos >= begin) & (kpos <= qpos)
            score = jnp.where(keep, score, -1e30)
            newmax = jnp.maximum(running, jnp.max(score, axis=1, keepdims=True))
            weight = jnp.exp2(score - newmax)
            factor = jnp.exp2(running - newmax)
            totals = totals * factor + jnp.sum(weight, axis=1, keepdims=True)
            accum = accum * factor + jnp.dot(
                weight.astype(jnp.bfloat16), vals[place, :], preferred_element_type=jnp.float32
            )
            return newmax, totals, accum

        state = (
            jnp.full((rows, 1), -1e30, jnp.float32),
            jnp.zeros((rows, 1), jnp.float32),
            jnp.zeros((rows, hsize), jnp.float32),
        )
        tiles = lax.div(after - lowest + KEYS - 1, KEYS)
        running, totals, accum = lax.fori_loop(0, tiles, tile, state)
        outs[m][...] = (accum / totals).astype(jnp.bfloat16)


def attend(where, starts, pieces):
    _, rows, hsize = pieces[0].shape
    scale = math.log2(math.e) / math.sqrt(hsize)
    return pl.pallas_call(
        functools.partial(attend_kernel, scale=scale),
        in_specs=[smem()] * 2 + [vmem()] * len(pieces),
        out_specs=[vmem()] * CHIPS,
        out_shape=[jax.ShapeDtypeStruct((rows, hsize), jnp.bfloat16)] * CHIPS,
        scratch_shapes=[pltpu.VMEM((KEYS + 2 * CHIPS * rows, hsize), jnp.bfloat16)] * 2,
        compiler_params=pltpu.CompilerParams(vmem_limit_bytes=16 << 20),
        cost_estimate=effort(16 * 2 * rows * LINE * rows * hsize),
        name="attend",
    )(where, starts, *pieces)


def early_kernel(where_ref, own, near, q1, p2, *refs):
    pieces, total_ref, last_ref, w_ref = refs[:10], refs[10], refs[11], refs[12]
    chip, core, line = where_ref[0], where_ref[1], where_ref[2]
    depth = pieces[0].shape[0]
    for side in range(2):
        for m in range(CHIPS):
            block = 2 * (chip ^ m) + (core if side == 0 else 1 - core)
            if m < 3:
                w_ref[block] = pieces[5 * side + m][...]
            else:
                w_ref[block, : depth // 2] = pieces[5 * side + 3][...]
                w_ref[block, depth // 2 :] = pieces[5 * side + 4][...]

    def term(block, feature):
        return jnp.dot(
            block[:, :depth], w_ref[2 * feature], preferred_element_type=jnp.float32
        ) + jnp.dot(block[:, depth:], w_ref[2 * feature + 1], preferred_element_type=jnp.float32)

    second, third, fourth, end = order(line)
    total = term(own[...], line) + term(near[...], second)
    total_ref[...] = total + term(jnp.where(end, p2[...], q1[...]), third)
    last_ref[:depth] = w_ref[2 * fourth]
    last_ref[depth:] = w_ref[2 * fourth + 1]


def early(where, blocks, pieces):
    rows, wide = blocks[0].shape
    depth, cols = pieces[0].shape
    return pl.pallas_call(
        early_kernel,
        in_specs=[smem()] + [vmem()] * (len(blocks) + len(pieces)),
        out_specs=[vmem()] * 2,
        out_shape=[
            jax.ShapeDtypeStruct((rows, cols), jnp.float32),
            jax.ShapeDtypeStruct((wide, cols), jnp.bfloat16),
        ],
        scratch_shapes=[pltpu.VMEM((2 * CHIPS, depth, cols), jnp.bfloat16)],
        compiler_params=pltpu.CompilerParams(vmem_limit_bytes=16 << 20),
        cost_estimate=effort(EARLY_EFFORT),
        name="early",
    )(where, *blocks, *pieces)


def last_kernel(where_ref, q2, p3, total_ref, w_ref, out_ref):
    end = order(where_ref[2])[3]
    block = jnp.where(end, p3[...], q2[...])
    total = total_ref[...] + jnp.dot(block, w_ref[...], preferred_element_type=jnp.float32)
    out_ref[...] = total.astype(jnp.bfloat16)


def last(where, q2, p3, total, w_last):
    return pl.pallas_call(
        last_kernel,
        in_specs=[smem()] + [vmem()] * 4,
        out_specs=vmem(),
        out_shape=jax.ShapeDtypeStruct(total.shape, jnp.bfloat16),
        compiler_params=pltpu.CompilerParams(vmem_limit_bytes=8 << 20),
        cost_estimate=effort(2 * total.shape[0] * w_last.size),
        name="last",
    )(where, q2, p3, total, w_last)


def heads_in_order(back, chip):
    odd, high = (chip & 1) == 1, (chip & 2) == 2
    low, top = [
        jnp.concatenate([jnp.where(odd, b, a), jnp.where(odd, a, b)], axis=1)
        for a, b in (back[:2], back[2:])
    ]
    return jnp.concatenate([jnp.where(high, top, low), jnp.where(high, low, top)], axis=1)


def together(*arrays):
    return lax.optimization_barrier(arrays)


def blocks_plan(tokens, gain, w_qkv, w_out, lengths):
    rows, wide = tokens.shape
    depth, _, heads, hsize = w_qkv.shape
    mine = lax.axis_index("gx")
    line = lax.axis_index("gy")
    chip, core = mine // 2, mine % 2
    where = jnp.stack([chip, core, line]).astype(jnp.int32)
    starts = (jnp.cumsum(lengths) - lengths).astype(jnp.int32)
    glob = mine * rows + jnp.arange(rows, dtype=jnp.int32)
    cosine, sine = tables(glob - begins(lengths, glob), hsize)
    cosine = jnp.concatenate([cosine, cosine], axis=1)
    sine = jnp.concatenate([-sine, sine], axis=1)

    flat = w_qkv.reshape(depth, -1)
    near, cosine, sine, where = together(outer(tokens), cosine, sine, where)
    q1 = inner(tokens)
    q2, p2 = inner(near), outward(q1)
    w_x, w_y = swap(flat, 2), swap(flat, 4)

    upper, lower = halves(w_x, w_y)
    p3, far_a, far_b = outward(q2), swap(upper, 2), swap(lower, 4)
    x = normalize(where, (tokens, near, q1, p2, q2, p3), gain.reshape(LINE, 1, wide))
    held = (flat, w_x, w_y, far_a, far_b)
    weights = held + tuple(swap(w, 1) for w in held)
    sent = [None] * CHIPS
    for pair in PAIRS:
        sent[pair[0]], sent[pair[1]] = project(where, pair, x, cosine, sine, weights)
    keys, vals = [heads_in_order([a[j] for a in sent], chip) for j in (1, 2)]

    pieces = [sent[0]] + [swap(sent[m], 2 * m) for m in range(1, CHIPS)]
    heads_out = attend(where, starts, pieces + [swap(a, 1) for a in pieces])
    back = [heads_out[0]] + [swap(heads_out[m], 2 * m) for m in range(1, CHIPS)]

    attended, w_late = together(heads_in_order(back, chip), w_out)
    near, q1 = outer(attended), inner(attended)
    w_x, w_y = swap(w_late, 2), swap(w_late, 4)
    upper, lower = halves(w_x, w_y)
    q1, upper, lower = together(q1, upper, lower)
    far_a, far_b = swap(upper, 2), swap(lower, 4)
    pieces = (w_late, w_x, w_y, far_a, far_b)
    q2, p2 = inner(near), outward(q1)
    p3 = outward(q2)
    pieces = pieces + tuple(swap(w, 1) for w in pieces)
    total, w_last = early(where, (attended, near, q1, p2), pieces)
    mixed = last(where, q2, p3, total, w_last)
    return (mixed, keys.reshape(rows, heads, hsize), vals.reshape(rows, heads, hsize))


def local(sizes, tokens, gain, w_qkv, w_out, lengths):
    heads = w_qkv.shape[2]
    fits = sizes == (2 * CHIPS, LINE) and heads == CHIPS and tokens.shape[1] == 2 * w_qkv.shape[0]
    plan = blocks_plan if fits else general
    return plan(tokens, gain, w_qkv, w_out, lengths)


def solution(mesh):
    sizes = (mesh.shape["gx"], mesh.shape["gy"])
    return jax.shard_map(
        functools.partial(local, sizes),
        mesh=mesh,
        in_specs=(P("gx", "gy"), P(), P("gx", None, "gy", None), P("gx", "gy"), P()),
        out_specs=(P("gx", "gy"), P("gx", "gy", None), P("gx", "gy", None)),
        check_vma=False,
    )
```

```python
import functools
import math

import jax
import jax.numpy as jnp
from jax import lax
from jax.experimental import pallas as pl
from jax.experimental.pallas import tpu as pltpu
from jax.sharding import PartitionSpec as P


def tables(position, hsize):
    half = hsize // 2
    freq = 10000.0 ** (-(2.0 * jnp.arange(half, dtype=jnp.float32)) / hsize)
    angle = position.astype(jnp.float32)[:, None] * freq[None, :]
    return jnp.cos(angle), jnp.sin(angle)


def rotate(vectors, position):
    half = vectors.shape[-1] // 2
    cosine, sine = tables(position, vectors.shape[-1])
    cosine, sine = cosine[:, None, :], sine[:, None, :]
    first = vectors[..., :half]
    second = vectors[..., half:]
    return jnp.concatenate(
        [first * cosine - second * sine, second * cosine + first * sine], axis=-1
    )


def begins(lengths, glob):
    doc_start = jnp.cumsum(lengths) - lengths
    return jnp.max(jnp.where(doc_start[None, :] <= glob[:, None], doc_start[None, :], 0), axis=1)


def block_rows(count):
    size = count
    while size > 1024 and size % 2 == 0:
        size = size // 2
    return size


def general(tokens, gain, w_qkv, w_out, lengths):
    tok_dev = tokens.shape[0]
    hloc = w_qkv.shape[2]
    hsize = w_qkv.shape[3]
    whole = lax.all_gather(tokens, "gy", axis=1, tiled=True)
    wide = whole.astype(jnp.float32)
    meansq = jnp.mean(wide * wide, axis=-1, keepdims=True)
    normed = (wide * lax.rsqrt(meansq + 1e-06) * gain[None, :]).astype(jnp.bfloat16)
    piece = lax.all_gather(w_qkv, "gx", axis=0, tiled=True)
    projected = jnp.dot(
        normed, piece.reshape(piece.shape[0], -1), preferred_element_type=jnp.float32
    )
    projected = projected.reshape(tok_dev, 3, hloc, hsize)
    mine = lax.axis_index("gx")
    glob = mine * tok_dev + jnp.arange(tok_dev, dtype=jnp.int32)
    begin = begins(lengths, glob)
    position = glob - begin
    query = rotate(projected[:, 0], position).astype(jnp.bfloat16)
    keys_own = rotate(projected[:, 1], position).astype(jnp.bfloat16)
    vals_own = projected[:, 2].astype(jnp.bfloat16)
    scale = 1.0 / math.sqrt(hsize)
    initial = (
        jnp.full((hloc, tok_dev), -1e30, jnp.float32),
        jnp.zeros((hloc, tok_dev), jnp.float32),
        jnp.zeros((hloc, tok_dev, hsize), jnp.float32),
    )
    keys_piece = lax.all_gather(keys_own, "gx", axis=0, tiled=True)
    vals_piece = lax.all_gather(vals_own, "gx", axis=0, tiled=True)
    count = keys_piece.shape[0]
    size = block_rows(count)

    def one_tile(number, state):
        running, totals, accum = state
        first = (number * size).astype(jnp.int32)
        keys_blk = lax.dynamic_slice_in_dim(keys_piece, first, size, 0)
        vals_blk = lax.dynamic_slice_in_dim(vals_piece, first, size, 0)
        kidx = first + jnp.arange(size, dtype=jnp.int32)
        score = (
            jnp.einsum("qhd,khd->hqk", query, keys_blk, preferred_element_type=jnp.float32) * scale
        )
        keep = (kidx[None, :] >= begin[:, None]) & (kidx[None, :] <= glob[:, None])
        score = jnp.where(keep[None], score, -1e30)
        newmax = jnp.maximum(running, jnp.max(score, axis=-1))
        weight = jnp.where(keep[None], jnp.exp(score - newmax[..., None]), 0.0)
        factor = jnp.exp(running - newmax)
        totals = totals * factor + jnp.sum(weight, axis=-1)
        update = jnp.einsum(
            "hqk,khd->hqd",
            weight.astype(jnp.bfloat16),
            vals_blk,
            preferred_element_type=jnp.float32,
        )
        accum = accum * factor[..., None] + update
        return (newmax, totals, accum)

    running, totals, accum = lax.fori_loop(0, count // size, one_tile, initial)
    attended = (accum / totals[..., None]).astype(jnp.bfloat16)
    attended = jnp.transpose(attended, (1, 0, 2)).reshape(tok_dev, hloc * hsize)
    all_heads = lax.all_gather(attended, "gy", axis=1, tiled=True)
    mixed = jnp.dot(
        all_heads, lax.all_gather(w_out, "gx", axis=0, tiled=True),
        preferred_element_type=jnp.float32,
    ).astype(jnp.bfloat16)
    return (mixed, keys_own, vals_own)


LINE = 4
CHIPS = 4
NORM_EFFORT = 8 << 30
PAIRS = ((1, 2), (3, 0))
KEYS = 512
EARLY_EFFORT = 1 << 30


def swap(x, mask):
    return lax.ppermute(x, "gx", [(i, i ^ mask) for i in range(2 * CHIPS)])


def outer(x):
    return lax.ppermute(x, "gy", [(0, 1), (1, 0), (2, 3), (3, 2)])


def inner(x):
    return lax.ppermute(x, "gy", [(1, 2), (2, 1)])


def outward(x):
    return lax.ppermute(x, "gy", [(1, 0), (2, 3)])


def order(line):
    low = line < 2
    return line ^ 1, jnp.where(low, 2, 1), jnp.where(low, 3, 0), (line == 0) | (line == LINE - 1)


def vmem():
    return pl.BlockSpec(memory_space=pltpu.VMEM)


def smem():
    return pl.BlockSpec(memory_space=pltpu.SMEM)


def hbm():
    return pl.BlockSpec(memory_space=pltpu.HBM)


def full(array):
    return pl.BlockSpec(array.shape, lambda *_: (0,) * array.ndim)


def effort(flops):
    return pl.CostEstimate(flops=flops, transcendentals=0, bytes_accessed=8 << 20)


def halves_kernel(x_ref, y_ref, upper_ref, lower_ref):
    upper_ref[...] = y_ref[...]
    lower_ref[...] = x_ref[...]


def halves(across, along):
    rows, cols = across.shape[0] // 2, across.shape[1]
    block = lambda half: pl.BlockSpec((rows, cols), lambda _: (half, 0))
    return pl.pallas_call(
        halves_kernel,
        grid=(1,),
        in_specs=[block(1), block(0)],
        out_specs=[block(0)] * 2,
        out_shape=[jax.ShapeDtypeStruct((rows, cols), across.dtype)] * 2,
        compiler_params=pltpu.CompilerParams(vmem_limit_bytes=6 << 20),
        name="halves",
    )(across, along)


def normalize_kernel(where_ref, *refs):
    blocks, (gain_ref, x_ref) = refs[:6], refs[6:]
    chip, line = where_ref[0], where_ref[2]
    wide = blocks[0].shape[1]
    own, near, q1, p2, q2, p3 = [block[...] for block in blocks]
    second, third, fourth, end = order(line)
    raw = [
        own.astype(jnp.float32),
        near.astype(jnp.float32),
        jnp.where(end, p2, q1).astype(jnp.float32),
        jnp.where(end, p3, q2).astype(jnp.float32),
    ]
    square = sum(jnp.sum(r * r, axis=1, keepdims=True) for r in raw)
    scale = lax.rsqrt(square * (1.0 / (LINE * wide)) + 1e-06)
    for r, feature in zip(raw, (line, second, third, fourth)):
        normed = (r * scale * gain_ref[feature]).astype(jnp.bfloat16)
        x_ref[:, pl.ds(pl.multiple_of((feature ^ chip) * wide, wide), wide)] = normed


def normalize(where, blocks, gain):
    rows, wide = blocks[0].shape
    return pl.pallas_call(
        normalize_kernel,
        in_specs=[smem()] + [vmem()] * 7,
        out_specs=vmem(),
        out_shape=jax.ShapeDtypeStruct((rows, LINE * wide), jnp.bfloat16),
        compiler_params=pltpu.CompilerParams(vmem_limit_bytes=12 << 20),
        cost_estimate=effort(NORM_EFFORT),
        name="normalize",
    )(where, *blocks, gain)


def head_columns(chip, pair, hsize):
    for i, m in enumerate(pair):
        for j in range(3):
            source = pl.multiple_of((CHIPS * j + (chip ^ m)) * hsize, hsize)
            yield pl.ds(source, hsize), slice((3 * i + j) * hsize, (3 * i + j + 1) * hsize)


def project_kernel(where_ref, x_ref, cos_ref, sin_ref, *refs, pair):
    weights, (out_a, out_b, w_ref) = refs[:10], refs[10:]
    chip, core = where_ref[0], where_ref[1]
    hsize = cos_ref.shape[1]
    depth = weights[0].shape[0]
    for source, target in head_columns(chip, pair, hsize):
        for side, half in ((0, core), (1, 1 - core)):
            for m in range(5):
                piece = weights[5 * side + m]
                row = (2 * min(m, 3) + half) * depth + (depth // 2 if m == 4 else 0)
                row = pl.multiple_of(row, depth // 2)
                w_ref[pl.ds(row, piece.shape[0]), target] = piece[:, source]
    total = jnp.dot(x_ref[...], w_ref[...], preferred_element_type=jnp.float32)
    for i, out in enumerate((out_a, out_b)):
        for j in range(3):
            u = total[:, (3 * i + j) * hsize : (3 * i + j + 1) * hsize]
            if j < 2:
                u = u * cos_ref[...] + pltpu.roll(u, hsize // 2, 1) * sin_ref[...]
            out[j] = u.astype(jnp.bfloat16)


def project(where, pair, x, cosine, sine, weights):
    rows, hsize = cosine.shape
    return pl.pallas_call(
        functools.partial(project_kernel, pair=pair),
        in_specs=[smem()] + [vmem()] * (3 + len(weights)),
        out_specs=[vmem()] * 2,
        out_shape=[jax.ShapeDtypeStruct((3, rows, hsize), jnp.bfloat16)] * 2,
        scratch_shapes=[pltpu.VMEM((x.shape[1], 6 * hsize), jnp.bfloat16)],
        compiler_params=pltpu.CompilerParams(vmem_limit_bytes=20 << 20),
        cost_estimate=effort(2 * x.size * 6 * hsize),
        name="project",
    )(where, x, cosine, sine, *weights)


def attend_kernel(where_ref, start_ref, *refs, scale):
    pieces, outs, (keys, vals) = refs[:8], refs[8:12], refs[12:]
    chip, core = where_ref[0], where_ref[1]
    _, rows, hsize = pieces[0].shape
    for cache in (keys, vals):
        cache[:KEYS] = jnp.zeros((KEYS, hsize), jnp.bfloat16)
    for side in range(2):
        for n in range(CHIPS):
            block = 2 * (chip ^ n) + (core if side == 0 else 1 - core)
            place = pl.ds(pl.multiple_of(KEYS + block * rows, 128), rows)
            keys[place, :] = pieces[CHIPS * side + n][1]
            vals[place, :] = pieces[CHIPS * side + n][2]
    for m in range(CHIPS):
        block = 2 * (chip ^ m) + core
        after = (block + 1) * rows
        query = pieces[m][0]
        qpos = block * rows + lax.broadcasted_iota(jnp.int32, (rows, 1), 0)
        begin = jnp.zeros((rows, 1), jnp.int32)
        lowest = jnp.int32(0)
        for d in range(start_ref.shape[0]):
            begin = jnp.where(start_ref[d] <= qpos, start_ref[d], begin)
            lowest = jnp.where(start_ref[d] <= block * rows, start_ref[d], lowest)

        def scores(number, after=after, query=query, begin=begin):
            first = after - KEYS * (number + 1)
            place = pl.ds(pl.multiple_of(KEYS + first, 128), KEYS)
            kpos = first + lax.broadcasted_iota(jnp.int32, (1, KEYS), 1)
            score = scale * lax.dot_general(
                query, keys[place, :], (((1,), (1,)), ((), ())), preferred_element_type=jnp.float32
            )
            return score, kpos, kpos >= begin, vals[place, :]

        def tile(number, state, scores=scores):
            running, totals, accum = state
            score, _, keep, values = scores(number)
            score = jnp.where(keep, score, -1e30)
            newmax = jnp.maximum(running, jnp.max(score, axis=1, keepdims=True))
            weight = jnp.exp2(score - newmax)
            factor = jnp.exp2(running - newmax)
            totals = totals * factor + jnp.sum(weight, axis=1, keepdims=True)
            accum = accum * factor + jnp.dot(
                weight.astype(jnp.bfloat16), values, preferred_element_type=jnp.float32
            )
            return newmax, totals, accum

        score, kpos, keep, values = scores(0)
        score = jnp.where(keep & (kpos <= qpos), score, -1e30)
        running = jnp.max(score, axis=1, keepdims=True)
        weight = jnp.exp2(score - running)
        totals = jnp.sum(weight, axis=1, keepdims=True)
        accum = jnp.dot(weight.astype(jnp.bfloat16), values, preferred_element_type=jnp.float32)
        tiles = lax.div(after - lowest + KEYS - 1, KEYS)
        running, totals, accum = lax.fori_loop(1, tiles, tile, (running, totals, accum))
        outs[m][...] = (accum / totals).astype(jnp.bfloat16)


def attend(where, starts, pieces):
    _, rows, hsize = pieces[0].shape
    scale = math.log2(math.e) / math.sqrt(hsize)
    return pl.pallas_call(
        functools.partial(attend_kernel, scale=scale),
        in_specs=[smem()] * 2 + [vmem()] * len(pieces),
        out_specs=[vmem()] * CHIPS,
        out_shape=[jax.ShapeDtypeStruct((rows, hsize), jnp.bfloat16)] * CHIPS,
        scratch_shapes=[pltpu.VMEM((KEYS + 2 * CHIPS * rows, hsize), jnp.bfloat16)] * 2,
        compiler_params=pltpu.CompilerParams(vmem_limit_bytes=16 << 20),
        cost_estimate=effort(16 * 2 * rows * LINE * rows * hsize),
        name="attend",
    )(where, starts, *pieces)


def early_kernel(where_ref, own, near, q1, p2, *refs):
    pieces, total_ref, last_ref, w_ref = refs[:10], refs[10], refs[11], refs[12]
    chip, core, line = where_ref[0], where_ref[1], where_ref[2]
    depth = pieces[0].shape[0]
    for side in range(2):
        for m in range(CHIPS):
            block = 2 * (chip ^ m) + (core if side == 0 else 1 - core)
            if m < 3:
                w_ref[block] = pieces[5 * side + m][...]
            else:
                w_ref[block, : depth // 2] = pieces[5 * side + 3][...]
                w_ref[block, depth // 2 :] = pieces[5 * side + 4][...]

    def term(block, feature):
        return jnp.dot(
            block[:, :depth], w_ref[2 * feature], preferred_element_type=jnp.float32
        ) + jnp.dot(block[:, depth:], w_ref[2 * feature + 1], preferred_element_type=jnp.float32)

    second, third, fourth, end = order(line)
    total = term(own[...], line) + term(near[...], second)
    total_ref[...] = total + term(jnp.where(end, p2[...], q1[...]), third)
    last_ref[:depth] = w_ref[2 * fourth]
    last_ref[depth:] = w_ref[2 * fourth + 1]


def early(where, blocks, pieces):
    rows, wide = blocks[0].shape
    depth, cols = pieces[0].shape
    return pl.pallas_call(
        early_kernel,
        in_specs=[smem()] + [vmem()] * (len(blocks) + len(pieces)),
        out_specs=[vmem()] * 2,
        out_shape=[
            jax.ShapeDtypeStruct((rows, cols), jnp.float32),
            jax.ShapeDtypeStruct((wide, cols), jnp.bfloat16),
        ],
        scratch_shapes=[pltpu.VMEM((2 * CHIPS, depth, cols), jnp.bfloat16)],
        compiler_params=pltpu.CompilerParams(vmem_limit_bytes=16 << 20),
        cost_estimate=effort(EARLY_EFFORT),
        name="early",
    )(where, *blocks, *pieces)


def last_kernel(where_ref, q2, p3, total_ref, w_ref, out_ref):
    end = order(where_ref[2])[3]
    block = jnp.where(end, p3[...], q2[...])
    total = total_ref[...] + jnp.dot(block, w_ref[...], preferred_element_type=jnp.float32)
    out_ref[...] = total.astype(jnp.bfloat16)


def last(where, q2, p3, total, w_last):
    return pl.pallas_call(
        last_kernel,
        in_specs=[smem()] + [vmem()] * 4,
        out_specs=vmem(),
        out_shape=jax.ShapeDtypeStruct(total.shape, jnp.bfloat16),
        compiler_params=pltpu.CompilerParams(vmem_limit_bytes=8 << 20),
        cost_estimate=effort(2 * total.shape[0] * w_last.size),
        name="last",
    )(where, q2, p3, total, w_last)


def heads_in_order(back, chip):
    odd, high = (chip & 1) == 1, (chip & 2) == 2
    low, top = [
        jnp.concatenate([jnp.where(odd, b, a), jnp.where(odd, a, b)], axis=1)
        for a, b in (back[:2], back[2:])
    ]
    return jnp.concatenate([jnp.where(high, top, low), jnp.where(high, low, top)], axis=1)


def together(*arrays):
    return lax.optimization_barrier(arrays)


def blocks_plan(tokens, gain, w_qkv, w_out, lengths):
    rows, wide = tokens.shape
    depth, _, heads, hsize = w_qkv.shape
    mine = lax.axis_index("gx")
    line = lax.axis_index("gy")
    chip, core = mine // 2, mine % 2
    where = jnp.stack([chip, core, line]).astype(jnp.int32)
    starts = (jnp.cumsum(lengths) - lengths).astype(jnp.int32)
    glob = mine * rows + jnp.arange(rows, dtype=jnp.int32)
    cosine, sine = tables(glob - begins(lengths, glob), hsize)
    cosine = jnp.concatenate([cosine, cosine], axis=1)
    sine = jnp.concatenate([-sine, sine], axis=1)

    flat = w_qkv.reshape(depth, -1)
    near, cosine, sine, where = together(outer(tokens), cosine, sine, where)
    q1 = inner(tokens)
    q2, p2 = inner(near), outward(q1)
    w_x, w_y = swap(flat, 2), swap(flat, 4)

    upper, lower = halves(w_x, w_y)
    p3, far_a, far_b = outward(q2), swap(upper, 2), swap(lower, 4)
    x = normalize(where, (tokens, near, q1, p2, q2, p3), gain.reshape(LINE, 1, wide))
    held = (flat, w_x, w_y, far_a, far_b)
    weights = held + tuple(swap(w, 1) for w in held)
    sent = [None] * CHIPS
    for pair in PAIRS:
        sent[pair[0]], sent[pair[1]] = project(where, pair, x, cosine, sine, weights)
    keys, vals = [heads_in_order([a[j] for a in sent], chip) for j in (1, 2)]

    pieces = [sent[0]] + [swap(sent[m], 2 * m) for m in range(1, CHIPS)]
    heads_out = attend(where, starts, pieces + [swap(a, 1) for a in pieces])
    back = [heads_out[0]] + [swap(heads_out[m], 2 * m) for m in range(1, CHIPS)]

    attended, w_late = together(heads_in_order(back, chip), w_out)
    near, q1 = outer(attended), inner(attended)
    w_x, w_y = swap(w_late, 2), swap(w_late, 4)
    upper, lower = halves(w_x, w_y)
    q1, upper, lower = together(q1, upper, lower)
    far_a, far_b = swap(upper, 2), swap(lower, 4)
    pieces = (w_late, w_x, w_y, far_a, far_b)
    q2, p2 = inner(near), outward(q1)
    p3 = outward(q2)
    pieces = pieces + tuple(swap(w, 1) for w in pieces)
    total, w_last = early(where, (attended, near, q1, p2), pieces)
    mixed = last(where, q2, p3, total, w_last)
    return (mixed, keys.reshape(rows, heads, hsize), vals.reshape(rows, heads, hsize))


def local(sizes, tokens, gain, w_qkv, w_out, lengths):
    heads = w_qkv.shape[2]
    fits = sizes == (2 * CHIPS, LINE) and heads == CHIPS and tokens.shape[1] == 2 * w_qkv.shape[0]
    fits = fits and tokens.shape[0] <= KEYS
    plan = blocks_plan if fits else general
    return plan(tokens, gain, w_qkv, w_out, lengths)


def solution(mesh):
    sizes = (mesh.shape["gx"], mesh.shape["gy"])
    return jax.shard_map(
        functools.partial(local, sizes),
        mesh=mesh,
        in_specs=(P("gx", "gy"), P(), P("gx", None, "gy", None), P("gx", "gy"), P()),
        out_specs=(P("gx", "gy"), P("gx", "gy", None), P("gx", "gy", None)),
        check_vma=False,
    )
```

```python
import functools
import math

import jax
import jax.numpy as jnp
from jax import lax
from jax.experimental import pallas as pl
from jax.experimental.pallas import tpu as pltpu
from jax.sharding import PartitionSpec as P


def tables(position, hsize):
    half = hsize // 2
    freq = 10000.0 ** (-(2.0 * jnp.arange(half, dtype=jnp.float32)) / hsize)
    angle = position.astype(jnp.float32)[:, None] * freq[None, :]
    return jnp.cos(angle), jnp.sin(angle)


def rotate(vectors, position):
    half = vectors.shape[-1] // 2
    cosine, sine = tables(position, vectors.shape[-1])
    cosine, sine = cosine[:, None, :], sine[:, None, :]
    first = vectors[..., :half]
    second = vectors[..., half:]
    return jnp.concatenate(
        [first * cosine - second * sine, second * cosine + first * sine], axis=-1
    )


def begins(lengths, glob):
    doc_start = jnp.cumsum(lengths) - lengths
    return jnp.max(jnp.where(doc_start[None, :] <= glob[:, None], doc_start[None, :], 0), axis=1)


def block_rows(count):
    size = count
    while size > 1024 and size % 2 == 0:
        size = size // 2
    return size


def general(tokens, gain, w_qkv, w_out, lengths):
    tok_dev = tokens.shape[0]
    hloc = w_qkv.shape[2]
    hsize = w_qkv.shape[3]
    whole = lax.all_gather(tokens, "gy", axis=1, tiled=True)
    wide = whole.astype(jnp.float32)
    meansq = jnp.mean(wide * wide, axis=-1, keepdims=True)
    normed = (wide * lax.rsqrt(meansq + 1e-06) * gain[None, :]).astype(jnp.bfloat16)
    piece = lax.all_gather(w_qkv, "gx", axis=0, tiled=True)
    projected = jnp.dot(
        normed, piece.reshape(piece.shape[0], -1), preferred_element_type=jnp.float32
    )
    projected = projected.reshape(tok_dev, 3, hloc, hsize)
    mine = lax.axis_index("gx")
    glob = mine * tok_dev + jnp.arange(tok_dev, dtype=jnp.int32)
    begin = begins(lengths, glob)
    position = glob - begin
    query = rotate(projected[:, 0], position).astype(jnp.bfloat16)
    keys_own = rotate(projected[:, 1], position).astype(jnp.bfloat16)
    vals_own = projected[:, 2].astype(jnp.bfloat16)
    scale = 1.0 / math.sqrt(hsize)
    initial = (
        jnp.full((hloc, tok_dev), -1e30, jnp.float32),
        jnp.zeros((hloc, tok_dev), jnp.float32),
        jnp.zeros((hloc, tok_dev, hsize), jnp.float32),
    )
    keys_piece = lax.all_gather(keys_own, "gx", axis=0, tiled=True)
    vals_piece = lax.all_gather(vals_own, "gx", axis=0, tiled=True)
    count = keys_piece.shape[0]
    size = block_rows(count)

    def one_tile(number, state):
        running, totals, accum = state
        first = (number * size).astype(jnp.int32)
        keys_blk = lax.dynamic_slice_in_dim(keys_piece, first, size, 0)
        vals_blk = lax.dynamic_slice_in_dim(vals_piece, first, size, 0)
        kidx = first + jnp.arange(size, dtype=jnp.int32)
        score = (
            jnp.einsum("qhd,khd->hqk", query, keys_blk, preferred_element_type=jnp.float32) * scale
        )
        keep = (kidx[None, :] >= begin[:, None]) & (kidx[None, :] <= glob[:, None])
        score = jnp.where(keep[None], score, -1e30)
        newmax = jnp.maximum(running, jnp.max(score, axis=-1))
        weight = jnp.where(keep[None], jnp.exp(score - newmax[..., None]), 0.0)
        factor = jnp.exp(running - newmax)
        totals = totals * factor + jnp.sum(weight, axis=-1)
        update = jnp.einsum(
            "hqk,khd->hqd",
            weight.astype(jnp.bfloat16),
            vals_blk,
            preferred_element_type=jnp.float32,
        )
        accum = accum * factor[..., None] + update
        return (newmax, totals, accum)

    running, totals, accum = lax.fori_loop(0, count // size, one_tile, initial)
    attended = (accum / totals[..., None]).astype(jnp.bfloat16)
    attended = jnp.transpose(attended, (1, 0, 2)).reshape(tok_dev, hloc * hsize)
    all_heads = lax.all_gather(attended, "gy", axis=1, tiled=True)
    mixed = jnp.dot(
        all_heads, lax.all_gather(w_out, "gx", axis=0, tiled=True),
        preferred_element_type=jnp.float32,
    ).astype(jnp.bfloat16)
    return (mixed, keys_own, vals_own)


LINE = 4
CHIPS = 4
NORM_EFFORT = 8 << 30
PAIRS = ((1, 2), (3, 0))
KEYS = 512
EARLY_EFFORT = 1 << 30


def swap(x, mask):
    return lax.ppermute(x, "gx", [(i, i ^ mask) for i in range(2 * CHIPS)])


def outer(x):
    return lax.ppermute(x, "gy", [(0, 1), (1, 0), (2, 3), (3, 2)])


def inner(x):
    return lax.ppermute(x, "gy", [(1, 2), (2, 1)])


def outward(x):
    return lax.ppermute(x, "gy", [(1, 0), (2, 3)])


def order(line):
    low = line < 2
    return line ^ 1, jnp.where(low, 2, 1), jnp.where(low, 3, 0), (line == 0) | (line == LINE - 1)


def vmem():
    return pl.BlockSpec(memory_space=pltpu.VMEM)


def smem():
    return pl.BlockSpec(memory_space=pltpu.SMEM)


def hbm():
    return pl.BlockSpec(memory_space=pltpu.HBM)


def full(array):
    return pl.BlockSpec(array.shape, lambda *_: (0,) * array.ndim)


def effort(flops):
    return pl.CostEstimate(flops=flops, transcendentals=0, bytes_accessed=8 << 20)


def halves_kernel(x_ref, y_ref, upper_ref, lower_ref):
    upper_ref[...] = y_ref[...]
    lower_ref[...] = x_ref[...]


def halves(across, along):
    rows, cols = across.shape[0] // 2, across.shape[1]
    block = lambda half: pl.BlockSpec((rows, cols), lambda _: (half, 0))
    return pl.pallas_call(
        halves_kernel,
        grid=(1,),
        in_specs=[block(1), block(0)],
        out_specs=[block(0)] * 2,
        out_shape=[jax.ShapeDtypeStruct((rows, cols), across.dtype)] * 2,
        compiler_params=pltpu.CompilerParams(vmem_limit_bytes=6 << 20),
        name="halves",
    )(across, along)


def normalize_kernel(where_ref, *refs):
    blocks, (gain_ref, x_ref) = refs[:6], refs[6:]
    chip, line = where_ref[0], where_ref[2]
    wide = blocks[0].shape[1]
    own, near, q1, p2, q2, p3 = [block[...] for block in blocks]
    second, third, fourth, end = order(line)
    raw = [
        own.astype(jnp.float32),
        near.astype(jnp.float32),
        jnp.where(end, p2, q1).astype(jnp.float32),
        jnp.where(end, p3, q2).astype(jnp.float32),
    ]
    square = sum(jnp.sum(r * r, axis=1, keepdims=True) for r in raw)
    scale = lax.rsqrt(square * (1.0 / (LINE * wide)) + 1e-06)
    for r, feature in zip(raw, (line, second, third, fourth)):
        normed = (r * scale * gain_ref[feature]).astype(jnp.bfloat16)
        x_ref[:, pl.ds(pl.multiple_of((feature ^ chip) * wide, wide), wide)] = normed


def normalize(where, blocks, gain):
    rows, wide = blocks[0].shape
    return pl.pallas_call(
        normalize_kernel,
        in_specs=[smem()] + [vmem()] * 7,
        out_specs=vmem(),
        out_shape=jax.ShapeDtypeStruct((rows, LINE * wide), jnp.bfloat16),
        compiler_params=pltpu.CompilerParams(vmem_limit_bytes=12 << 20),
        cost_estimate=effort(NORM_EFFORT),
        name="normalize",
    )(where, *blocks, gain)


def head_columns(chip, pair, hsize):
    for i, m in enumerate(pair):
        for j in range(3):
            source = pl.multiple_of((CHIPS * j + (chip ^ m)) * hsize, hsize)
            yield pl.ds(source, hsize), slice((3 * i + j) * hsize, (3 * i + j + 1) * hsize)


def project_kernel(where_ref, x_ref, cos_ref, sin_ref, *refs, pair):
    weights, (out_a, out_b, w_ref) = refs[:10], refs[10:]
    chip, core = where_ref[0], where_ref[1]
    hsize = cos_ref.shape[1]
    depth = weights[0].shape[0]
    for source, target in head_columns(chip, pair, hsize):
        for side, half in ((0, core), (1, 1 - core)):
            for m in range(5):
                piece = weights[5 * side + m]
                row = (2 * min(m, 3) + half) * depth + (depth // 2 if m == 4 else 0)
                row = pl.multiple_of(row, depth // 2)
                w_ref[pl.ds(row, piece.shape[0]), target] = piece[:, source]
    total = jnp.dot(x_ref[...], w_ref[...], preferred_element_type=jnp.float32)
    for i, out in enumerate((out_a, out_b)):
        for j in range(3):
            u = total[:, (3 * i + j) * hsize : (3 * i + j + 1) * hsize]
            if j < 2:
                u = u * cos_ref[...] + pltpu.roll(u, hsize // 2, 1) * sin_ref[...]
            out[j] = u.astype(jnp.bfloat16)


def project(where, pair, x, cosine, sine, weights):
    rows, hsize = cosine.shape
    return pl.pallas_call(
        functools.partial(project_kernel, pair=pair),
        in_specs=[smem()] + [vmem()] * (3 + len(weights)),
        out_specs=[vmem()] * 2,
        out_shape=[jax.ShapeDtypeStruct((3, rows, hsize), jnp.bfloat16)] * 2,
        scratch_shapes=[pltpu.VMEM((x.shape[1], 6 * hsize), jnp.bfloat16)],
        compiler_params=pltpu.CompilerParams(vmem_limit_bytes=20 << 20),
        cost_estimate=effort(2 * x.size * 6 * hsize),
        name="project",
    )(where, x, cosine, sine, *weights)


def attend_kernel(where_ref, start_ref, *refs, scale):
    pieces, outs, (keys, vals) = refs[:8], refs[8:12], refs[12:]
    chip, core = where_ref[0], where_ref[1]
    _, rows, hsize = pieces[0].shape
    for cache in (keys, vals):
        cache[:KEYS] = jnp.zeros((KEYS, hsize), jnp.bfloat16)
    for side in range(2):
        for n in range(CHIPS):
            block = 2 * (chip ^ n) + (core if side == 0 else 1 - core)
            place = pl.ds(pl.multiple_of(KEYS + block * rows, 128), rows)
            keys[place, :] = pieces[CHIPS * side + n][1]
            vals[place, :] = pieces[CHIPS * side + n][2]
    for m in range(CHIPS):
        block = 2 * (chip ^ m) + core
        after = (block + 1) * rows
        query = pieces[m][0]
        qpos = block * rows + lax.broadcasted_iota(jnp.int32, (rows, 1), 0)
        begin = jnp.zeros((rows, 1), jnp.int32)
        lowest = highest = jnp.int32(0)
        for d in range(start_ref.shape[0]):
            begin = jnp.where(start_ref[d] <= qpos, start_ref[d], begin)
            lowest = jnp.where(start_ref[d] <= block * rows, start_ref[d], lowest)
            highest = jnp.where(start_ref[d] < after, start_ref[d], highest)

        def scores(number, after=after, query=query, begin=begin):
            first = after - KEYS * (number + 1)
            place = pl.ds(pl.multiple_of(KEYS + first, 128), KEYS)
            kpos = first + lax.broadcasted_iota(jnp.int32, (1, KEYS), 1)
            score = scale * lax.dot_general(
                query, keys[place, :], (((1,), (1,)), ((), ())), preferred_element_type=jnp.float32
            )
            return score, kpos, kpos >= begin, vals[place, :]

        def tile(number, state, scores=scores, masked=True):
            running, totals, accum = state
            score, _, keep, values = scores(number)
            if masked:
                score = jnp.where(keep, score, -1e30)
            newmax = jnp.maximum(running, jnp.max(score, axis=1, keepdims=True))
            weight = jnp.exp2(score - newmax)
            factor = jnp.exp2(running - newmax)
            totals = totals * factor + jnp.sum(weight, axis=1, keepdims=True)
            accum = accum * factor + jnp.dot(
                weight.astype(jnp.bfloat16), values, preferred_element_type=jnp.float32
            )
            return newmax, totals, accum

        score, kpos, keep, values = scores(0)
        score = jnp.where(keep & (kpos <= qpos), score, -1e30)
        running = jnp.max(score, axis=1, keepdims=True)
        weight = jnp.exp2(score - running)
        totals = jnp.sum(weight, axis=1, keepdims=True)
        accum = jnp.dot(weight.astype(jnp.bfloat16), values, preferred_element_type=jnp.float32)
        tiles = lax.div(after - lowest + KEYS - 1, KEYS)
        whole = jnp.maximum(lax.div(after - highest, KEYS), 1)
        state = (running, totals, accum)
        state = lax.fori_loop(1, whole, functools.partial(tile, masked=False), state)
        running, totals, accum = lax.fori_loop(whole, tiles, tile, state)
        outs[m][...] = (accum / totals).astype(jnp.bfloat16)


def attend(where, starts, pieces):
    _, rows, hsize = pieces[0].shape
    scale = math.log2(math.e) / math.sqrt(hsize)
    return pl.pallas_call(
        functools.partial(attend_kernel, scale=scale),
        in_specs=[smem()] * 2 + [vmem()] * len(pieces),
        out_specs=[vmem()] * CHIPS,
        out_shape=[jax.ShapeDtypeStruct((rows, hsize), jnp.bfloat16)] * CHIPS,
        scratch_shapes=[pltpu.VMEM((KEYS + 2 * CHIPS * rows, hsize), jnp.bfloat16)] * 2,
        compiler_params=pltpu.CompilerParams(vmem_limit_bytes=16 << 20),
        cost_estimate=effort(16 * 2 * rows * LINE * rows * hsize),
        name="attend",
    )(where, starts, *pieces)


def early_kernel(where_ref, own, near, q1, p2, *refs):
    pieces, total_ref, last_ref, w_ref = refs[:10], refs[10], refs[11], refs[12]
    chip, core, line = where_ref[0], where_ref[1], where_ref[2]
    depth = pieces[0].shape[0]
    for side in range(2):
        for m in range(CHIPS):
            block = 2 * (chip ^ m) + (core if side == 0 else 1 - core)
            if m < 3:
                w_ref[block] = pieces[5 * side + m][...]
            else:
                w_ref[block, : depth // 2] = pieces[5 * side + 3][...]
                w_ref[block, depth // 2 :] = pieces[5 * side + 4][...]

    def term(block, feature):
        return jnp.dot(
            block[:, :depth], w_ref[2 * feature], preferred_element_type=jnp.float32
        ) + jnp.dot(block[:, depth:], w_ref[2 * feature + 1], preferred_element_type=jnp.float32)

    second, third, fourth, end = order(line)
    total = term(own[...], line) + term(near[...], second)
    total_ref[...] = total + term(jnp.where(end, p2[...], q1[...]), third)
    last_ref[:depth] = w_ref[2 * fourth]
    last_ref[depth:] = w_ref[2 * fourth + 1]


def early(where, blocks, pieces):
    rows, wide = blocks[0].shape
    depth, cols = pieces[0].shape
    return pl.pallas_call(
        early_kernel,
        in_specs=[smem()] + [vmem()] * (len(blocks) + len(pieces)),
        out_specs=[vmem()] * 2,
        out_shape=[
            jax.ShapeDtypeStruct((rows, cols), jnp.float32),
            jax.ShapeDtypeStruct((wide, cols), jnp.bfloat16),
        ],
        scratch_shapes=[pltpu.VMEM((2 * CHIPS, depth, cols), jnp.bfloat16)],
        compiler_params=pltpu.CompilerParams(vmem_limit_bytes=16 << 20),
        cost_estimate=effort(EARLY_EFFORT),
        name="early",
    )(where, *blocks, *pieces)


def last_kernel(where_ref, q2, p3, total_ref, w_ref, out_ref):
    end = order(where_ref[2])[3]
    block = jnp.where(end, p3[...], q2[...])
    total = total_ref[...] + jnp.dot(block, w_ref[...], preferred_element_type=jnp.float32)
    out_ref[...] = total.astype(jnp.bfloat16)


def last(where, q2, p3, total, w_last):
    return pl.pallas_call(
        last_kernel,
        in_specs=[smem()] + [vmem()] * 4,
        out_specs=vmem(),
        out_shape=jax.ShapeDtypeStruct(total.shape, jnp.bfloat16),
        compiler_params=pltpu.CompilerParams(vmem_limit_bytes=8 << 20),
        cost_estimate=effort(2 * total.shape[0] * w_last.size),
        name="last",
    )(where, q2, p3, total, w_last)


def heads_in_order(back, chip):
    odd, high = (chip & 1) == 1, (chip & 2) == 2
    low, top = [
        jnp.concatenate([jnp.where(odd, b, a), jnp.where(odd, a, b)], axis=1)
        for a, b in (back[:2], back[2:])
    ]
    return jnp.concatenate([jnp.where(high, top, low), jnp.where(high, low, top)], axis=1)


def together(*arrays):
    return lax.optimization_barrier(arrays)


def blocks_plan(tokens, gain, w_qkv, w_out, lengths):
    rows, wide = tokens.shape
    depth, _, heads, hsize = w_qkv.shape
    mine = lax.axis_index("gx")
    line = lax.axis_index("gy")
    chip, core = mine // 2, mine % 2
    where = jnp.stack([chip, core, line]).astype(jnp.int32)
    starts = (jnp.cumsum(lengths) - lengths).astype(jnp.int32)
    glob = mine * rows + jnp.arange(rows, dtype=jnp.int32)
    cosine, sine = tables(glob - begins(lengths, glob), hsize)
    cosine = jnp.concatenate([cosine, cosine], axis=1)
    sine = jnp.concatenate([-sine, sine], axis=1)

    flat = w_qkv.reshape(depth, -1)
    near, cosine, sine, where = together(outer(tokens), cosine, sine, where)
    q1 = inner(tokens)
    q2, p2 = inner(near), outward(q1)
    w_x, w_y = swap(flat, 2), swap(flat, 4)

    upper, lower = halves(w_x, w_y)
    p3, far_a, far_b = outward(q2), swap(upper, 2), swap(lower, 4)
    x = normalize(where, (tokens, near, q1, p2, q2, p3), gain.reshape(LINE, 1, wide))
    held = (flat, w_x, w_y, far_a, far_b)
    weights = held + tuple(swap(w, 1) for w in held)
    sent = [None] * CHIPS
    for pair in PAIRS:
        sent[pair[0]], sent[pair[1]] = project(where, pair, x, cosine, sine, weights)
    keys, vals = [heads_in_order([a[j] for a in sent], chip) for j in (1, 2)]

    pieces = [sent[0]] + [swap(sent[m], 2 * m) for m in range(1, CHIPS)]
    heads_out = attend(where, starts, pieces + [swap(a, 1) for a in pieces])
    back = [heads_out[0]] + [swap(heads_out[m], 2 * m) for m in range(1, CHIPS)]

    attended, w_late = together(heads_in_order(back, chip), w_out)
    near, q1 = outer(attended), inner(attended)
    w_x, w_y = swap(w_late, 2), swap(w_late, 4)
    upper, lower = halves(w_x, w_y)
    q1, upper, lower = together(q1, upper, lower)
    far_a, far_b = swap(upper, 2), swap(lower, 4)
    pieces = (w_late, w_x, w_y, far_a, far_b)
    q2, p2 = inner(near), outward(q1)
    p3 = outward(q2)
    pieces = pieces + tuple(swap(w, 1) for w in pieces)
    total, w_last = early(where, (attended, near, q1, p2), pieces)
    mixed = last(where, q2, p3, total, w_last)
    return (mixed, keys.reshape(rows, heads, hsize), vals.reshape(rows, heads, hsize))


def local(sizes, tokens, gain, w_qkv, w_out, lengths):
    heads = w_qkv.shape[2]
    fits = sizes == (2 * CHIPS, LINE) and heads == CHIPS and tokens.shape[1] == 2 * w_qkv.shape[0]
    fits = fits and tokens.shape[0] <= KEYS
    plan = blocks_plan if fits else general
    return plan(tokens, gain, w_qkv, w_out, lengths)


def solution(mesh):
    sizes = (mesh.shape["gx"], mesh.shape["gy"])
    return jax.shard_map(
        functools.partial(local, sizes),
        mesh=mesh,
        in_specs=(P("gx", "gy"), P(), P("gx", None, "gy", None), P("gx", "gy"), P()),
        out_specs=(P("gx", "gy"), P("gx", "gy", None), P("gx", "gy", None)),
        check_vma=False,
    )
```
